256 devices in a mesh: px: 4 (over y_lo, core), py: 8 (over x, y_hi), dom: 8 (over z).
Axes of the slice: x: 4, y: 4 (y_hi: 2, y_lo: 2; y = y_hi * 2 + y_lo), z: 8, core: 2. Of those that a mesh axis runs over, the one named last changes fastest.
Arguments:
- velocity: float32 [16, 64, 256, 128], P('dom', 'px', 'py'), may hold values from 0.65 to 2.2
- buoyancy: float32 [64, 256, 128], P('px', 'py'), may hold values from 0.6 to 1.6
- forward_prev: float32 [16, 64, 256, 128], P('dom', 'px', 'py'), may hold values from -12 to 12
- forward_now: float32 [16, 64, 256, 128], P('dom', 'px', 'py'), may hold values from -12 to 12
- adjoint_prev: float32 [16, 64, 256, 128], P('dom', 'px', 'py'), may hold values from -12 to 12
- adjoint_now: float32 [16, 64, 256, 128], P('dom', 'px', 'py'), may hold values from -12 to 12
- sources: int32 [16], P('dom'), may hold values from 0 to 2097151
- wavelet: float32 [16, 3], P('dom'), may hold values from -800 to 800
- receivers: int32 [16, 1024], P('dom'), may hold values from 0 to 2097151
- misfit: float32 [16, 3, 1024], P('dom'), may hold values from -6 to 6
- sponge: int32 [6], replicated, may hold values from 2 to 8
Outputs:
- forward_before: float32 [16, 64, 256, 128], P('dom', 'px', 'py')
- forward_after: float32 [16, 64, 256, 128], P('dom', 'px', 'py')
- adjoint_before: float32 [16, 64, 256, 128], P('dom', 'px', 'py')
- adjoint_after: float32 [16, 64, 256, 128], P('dom', 'px', 'py')
- drift: float32 [16, 64, 256, 128], P('dom', 'px', 'py')
- spread: float32 [16, 64, 256, 128], P('dom', 'px', 'py')
The draws below stay inside these ranges and needn't reach their ends.
All inputs are finite; a program needn't handle non-finite values.
Results may differ from the reference program's by a relative error of at most 0.0003.
Values sent between devices are 32-bit elements; how exact they have to be, the bound alone decides.
A program may use at most 64 MiB of HBM per device.

```python
import math
import jax
import jax.numpy as jnp
from jax import lax

CX = 16
CY = 32
STEPS = 3
RECV = 1024
PARTICLES = 16
NX = 64
NY = 256
NZ = 128


def draw_velocity(key, part):
    key_amp, key_cell = jax.random.split(jax.random.fold_in(key, 101))
    log_amp = jax.random.uniform(key_amp, (PARTICLES, NX // CX, NY // CY), minval=jnp.log(0.05), maxval=jnp.log(0.3))
    amplitude = jnp.repeat(jnp.repeat(jnp.exp(log_amp), CX, axis=1), CY, axis=2)[..., None]
    noise = jnp.clip(jax.random.normal(key_cell, (PARTICLES, NX, NY, NZ)), -2.0, 2.0)
    return 1.2 * jnp.exp(amplitude * noise)


def wave_draw(key, tag):
    key_cell = jax.random.fold_in(key, tag)
    along_x = jnp.arange(NX, dtype=jnp.float32) / NX
    along_y = jnp.arange(NY, dtype=jnp.float32) / NY
    envelope = 3.0 ** (0.5 * along_x[:, None] + 0.5 * along_y[None, :])
    noise = jnp.clip(jax.random.normal(key_cell, (PARTICLES, NX, NY, NZ)), -4.0, 4.0)
    return envelope[None, :, :, None] * noise


def draw_forward_prev(key, part):
    return wave_draw(key, 211)


def draw_forward_now(key, part):
    return wave_draw(key, 223)


def draw_adjoint_prev(key, part):
    return wave_draw(key, 227)


def draw_adjoint_now(key, part):
    return wave_draw(key, 229)


def plant(drawn, key, least, high):
    shape = drawn.shape
    place = [jax.random.randint(jax.random.fold_in(key, axis), (), 0, shape[axis]) for axis in range(len(shape))]
    drawn = drawn.at[tuple(place)].set(least)
    longest = shape.index(max(shape))
    place[longest] = (place[longest] + 1) % shape[longest]
    return drawn.at[tuple(place)].set(high)


def block_scale(stream_key, shape, pieces, low, top_value):
    def one(axis_at, parts):
        steps = jax.random.uniform(jax.random.fold_in(jax.random.fold_in(stream_key, 6), axis_at), (parts,), jnp.float32, low / len(pieces), top_value / len(pieces))
        return jnp.repeat(jnp.exp(steps), shape[axis_at] // parts).reshape((-1,) + (1,) * (len(shape) - axis_at - 1))

    loudness = one(*pieces[0])
    for cut in pieces[1:]:
        loudness = loudness * one(*cut)
    return loudness


def setup_inputs(seed: int = 0) -> dict:
    keys = jax.random.split(jax.random.key(seed), 12)
    return {
        "velocity": draw_velocity(jax.random.fold_in(keys[11], 71), 0),
        "buoyancy": jnp.clip(jnp.exp(math.log(1.6) - 0.98082923 * jax.random.uniform(keys[1], (NX, NY, NZ), jnp.float32) ** block_scale(keys[1], (NX, NY, NZ), ((0, 4), (1, 8)), -0.2, 0.2)), 0.6, 1.6),
        "forward_prev": draw_forward_prev(jax.random.fold_in(keys[11], 71), 0),
        "forward_now": draw_forward_now(jax.random.fold_in(keys[11], 71), 0),
        "adjoint_prev": draw_adjoint_prev(jax.random.fold_in(keys[11], 71), 0),
        "adjoint_now": draw_adjoint_now(jax.random.fold_in(keys[11], 71), 0),
        "sources": plant(jax.random.randint(keys[6], (PARTICLES,), 0, NX * NY * NZ), jax.random.fold_in(keys[6], 1), 0, (NX * NY * NZ) - 1).astype(jnp.int32),
        "wavelet": jnp.clip(jax.random.uniform(keys[7], (PARTICLES, STEPS), jnp.float32, -800.0, 800.0) * block_scale(keys[7], (PARTICLES, STEPS), ((0, 8),), -0.4, 0.0), -800.0, 800.0),
        "receivers": plant(jax.random.randint(keys[8], (PARTICLES, RECV), 0, NX * NY * NZ), jax.random.fold_in(keys[8], 1), 0, (NX * NY * NZ) - 1).astype(jnp.int32),
        "misfit": jnp.clip(jax.random.uniform(keys[9], (PARTICLES, STEPS, RECV), jnp.float32, -6.0, 6.0) * block_scale(keys[9], (PARTICLES, STEPS, RECV), ((0, 8),), -0.4, 0.0), -6.0, 6.0),
        "sponge": plant(jax.random.randint(keys[10], (6,), 2, 9), jax.random.fold_in(keys[10], 1), 2, 8).astype(jnp.int32),
    }


EPSILON = 1e-06
TIME_STEP = 0.18
SPONGE_RATE = 0.5
NEAR_WEIGHT = 9.0 / 8.0
FAR_WEIGHT = 1.0 / 24.0

def take_slab(source_array, start_at, amount, which_axis):
    return lax.slice_in_dim(source_array, start_at, start_at + amount, axis=source_array.ndim + which_axis)

def axis_term(wave_field, buoy_field, extent, which_axis):
    half_buoy = 0.5 * (take_slab(buoy_field, 1, extent + 3, which_axis) + take_slab(buoy_field, 2, extent + 3, which_axis))
    slope_face = NEAR_WEIGHT * (take_slab(wave_field, 2, extent + 3, which_axis) - take_slab(wave_field, 1, extent + 3, which_axis)) - FAR_WEIGHT * (take_slab(wave_field, 3, extent + 3, which_axis) - take_slab(wave_field, 0, extent + 3, which_axis))
    flux_face = half_buoy * slope_face
    return NEAR_WEIGHT * (take_slab(flux_face, 2, extent, which_axis) - take_slab(flux_face, 1, extent, which_axis)) - FAR_WEIGHT * (take_slab(flux_face, 3, extent, which_axis) - take_slab(flux_face, 0, extent, which_axis))

def divergence(padded, buoy_pad):
    size_x = padded.shape[-3] - 6
    size_y = padded.shape[-2] - 6
    size_z = padded.shape[-1] - 6
    along_x = axis_term(padded[..., 3:size_y + 3, 3:size_z + 3], buoy_pad[:, 3:size_y + 3, 3:size_z + 3], size_x, -3)
    along_y = axis_term(padded[..., 3:size_x + 3, :, 3:size_z + 3], buoy_pad[3:size_x + 3, :, 3:size_z + 3], size_y, -2)
    along_z = axis_term(padded[..., 3:size_x + 3, 3:size_y + 3, :], buoy_pad[3:size_x + 3, 3:size_y + 3, :], size_z, -1)
    return along_x + along_y + along_z

def sponge_term(coords, length, low_width, high_width):
    position = coords.astype(jnp.float32)
    far_side = length - 1 - position
    low_float = low_width.astype(jnp.float32)
    high_float = high_width.astype(jnp.float32)
    low_part = jnp.where(position < low_float, jnp.square(SPONGE_RATE * (low_float - position) / low_float), 0.0)
    high_part = jnp.where(far_side < high_float, jnp.square(SPONGE_RATE * (high_float - far_side) / high_float), 0.0)
    return low_part + high_part

def reference(velocity, buoyancy, forward_prev, forward_now, adjoint_prev, adjoint_now, sources, wavelet, receivers, misfit, sponge):
    step_sq = TIME_STEP * TIME_STEP
    damping = jnp.exp(-(sponge_term(jnp.arange(NX, dtype=jnp.int32), NX, sponge[0], sponge[1])[:, None, None] + sponge_term(jnp.arange(NY, dtype=jnp.int32), NY, sponge[2], sponge[3])[None, :, None] + sponge_term(jnp.arange(NZ, dtype=jnp.int32), NZ, sponge[4], sponge[5])[None, None, :]))
    buoy_pad = jnp.pad(buoyancy, 3)

    def one_particle(items):
        model_block, fwd_before, fwd_now, adj_before, adj_now, source_cell, wave_row, receiver_row, misfit_block = items
        wave_scale = model_block * model_block / buoyancy
        grad_coef = -2.0 / (model_block * model_block * model_block)
        previous = jnp.stack([fwd_before, adj_before])
        current = jnp.stack([fwd_now, adj_now])
        gradient = jnp.zeros_like(model_block)
        for step_at in range(STEPS):
            padded = jnp.pad(current, ((0, 0), (3, 3), (3, 3), (3, 3)))
            stepped = 2.0 * current - previous + step_sq * (wave_scale * divergence(padded, buoy_pad))
            flat_waves = stepped.reshape(2, NX * NY * NZ)
            flat_waves = flat_waves.at[0, source_cell].add(step_sq * wave_row[step_at])
            flat_waves = flat_waves.at[1, receiver_row].add(step_sq * misfit_block[step_at])
            advanced = damping * flat_waves.reshape(stepped.shape)
            gradient = gradient + grad_coef * current[1] * (advanced[0] - 2.0 * current[0] + previous[0])
            previous, current = (current, advanced)
        return (previous, current, gradient)
    previous, current, gradient = lax.map(one_particle, (velocity, forward_prev, forward_now, adjoint_prev, adjoint_now, sources, wavelet, receivers, misfit))
    flat_grad = gradient.reshape(PARTICLES, NX * NY * NZ)
    norms = jnp.sqrt(lax.optimization_barrier(jnp.sum(flat_grad * flat_grad, axis=1)) / (NX * NY * NZ) + EPSILON)
    unit_grad = flat_grad / norms[:, None]
    flat_model = velocity.reshape(PARTICLES, NX * NY * NZ)

    def row_distance(model_row):
        difference = flat_model - model_row[None, :]
        return lax.optimization_barrier(jnp.sum(difference * difference, axis=1))
    dist_sq = lax.map(row_distance, flat_model)
    width = jnp.sum(dist_sq) / (PARTICLES * (PARTICLES - 1)) + EPSILON
    kernel = jnp.exp(-dist_sq / width)
    row_sum = lax.optimization_barrier(jnp.sum(kernel, axis=1))
    drift = jnp.dot(kernel, unit_grad, precision=lax.Precision.HIGHEST, preferred_element_type=jnp.float32)
    model_mix = jnp.dot(kernel, flat_model, precision=lax.Precision.HIGHEST, preferred_element_type=jnp.float32)
    spread = flat_model * row_sum[:, None] - model_mix
    full_shape = velocity.shape
    return (previous[:, 0], current[:, 0], previous[:, 1], current[:, 1], drift.reshape(full_shape), spread.reshape(full_shape))
```

```python
import functools

import jax
import jax.numpy as jnp
from jax import lax
from jax.experimental import pallas as pl
from jax.experimental.pallas import tpu as pltpu
from jax.sharding import PartitionSpec as P

EPSILON = 1e-06
TIME_STEP = 0.18
STEP_SQ = TIME_STEP * TIME_STEP
SPONGE_RATE = 0.5
NEAR = 9.0 / 8.0
FAR = 1.0 / 24.0
MESH = pl.DeviceIdType.MESH
F32 = jnp.float32
BF16 = jnp.bfloat16
HIGHEST = lax.Precision.HIGHEST
NT = (((1,), (1,)), ((), ()))
EDGE = 3
TOP = 8


def sponge_part(position, length, low, high):
    far_side = (length - 1) - position
    low_part = jnp.where(position < low, jnp.square(SPONGE_RATE * (low - position) / low), 0.0)
    high_part = jnp.where(far_side < high, jnp.square(SPONGE_RATE * (high - far_side) / high), 0.0)
    return low_part + high_part


def axis_coefs(faces):
    below2, below, here, above = faces
    near_sq, cross, far_sq = NEAR * NEAR, NEAR * FAR, FAR * FAR
    return (
        -near_sq * (here + below) - far_sq * (above + below2),
        near_sq * here + cross * (below + above),
        near_sq * below + cross * (here + below2),
        -cross * (here + above),
        -cross * (below + below2),
        far_sq * above,
        far_sq * below2,
    )


SHIFTS = (1, -1, 2, -2, 3, -3)


def kernel(
    counts,
    vel_in,
    buoy_in,
    fp_in,
    fn_in,
    ap_in,
    an_in,
    sources,
    wavelet,
    receivers,
    misfit,
    sponge,
    fb_out,
    fa_out,
    ab_out,
    aa_out,
    drift_out,
    spread_out,
    S,
    vel,
    bpad,
    C,
    damp,
    src_hot,
    inj,
    b_hi,
    b_lo,
    grad,
    mcols,
    gcols,
    mix_m,
    mix_g,
    T,
    KB,
    gram_px,
    gram_py,
    gram_dom,
    norm_px,
    norm_py,
    norm_dom,
    load_sem,
    halo_send,
    halo_recv,
    col_send,
    col_recv,
    sum_send,
    sum_recv,
    out_sem,
):
    n_px, n_py, n_dom = counts
    parts, size_x, size_y, size_z = vel.shape
    steps = wavelet.shape[1]
    tiles = size_y // 8
    px, py, dom = lax.axis_index("px"), lax.axis_index("py"), lax.axis_index("dom")
    coord = {"px": px, "py": py, "dom": dom}
    count = {"px": n_px, "py": n_py, "dom": n_dom}
    total_x, total_y = size_x * n_px, size_y * n_py
    particles = parts * n_dom
    share = size_x // n_dom
    cells = pl.ds(EDGE, size_x), pl.ds(TOP, size_y)
    row8 = lax.broadcasted_iota(jnp.int32, (8, size_z), 0)
    lane8 = lax.broadcasted_iota(jnp.int32, (8, size_z), 1)

    def peer(axis, k):
        return lax.rem(coord[axis] + k, count[axis])

    barrier = pltpu.get_barrier_semaphore()
    for axis in ("px", "py", "dom"):
        for k in range(1, count[axis]):
            pl.semaphore_signal(barrier, inc=1, device_id={axis: peer(axis, k)}, device_id_type=MESH)

    loads = [
        pltpu.make_async_copy(vel_in, vel, load_sem.at[0]),
        pltpu.make_async_copy(buoy_in, bpad.at[cells], load_sem.at[1]),
        pltpu.make_async_copy(fn_in, S.at[(1, pl.ds(0, parts)) + cells], load_sem.at[2]),
        pltpu.make_async_copy(an_in, S.at[(1, pl.ds(parts, parts)) + cells], load_sem.at[3]),
        pltpu.make_async_copy(fp_in, S.at[(0, pl.ds(0, parts)) + cells], load_sem.at[4]),
        pltpu.make_async_copy(ap_in, S.at[(0, pl.ds(parts, parts)) + cells], load_sem.at[5]),
    ]
    for copy in loads:
        copy.start()

    zero_rows = jnp.zeros((8, size_z), F32)
    zero_plane = jnp.zeros((size_y, size_z), F32)

    def zero_planes(first):
        for k in range(EDGE):
            bpad[first + k, pl.ds(TOP, size_y), :] = zero_plane
            for state in range(1, 1 + steps):
                for f in range(2 * parts):
                    S[state, f, first + k, pl.ds(TOP, size_y), :] = zero_plane

    def zero_strip(first):
        def body(x, carry):
            bpad[x, pl.ds(first, 8), :] = zero_rows
            for state in range(1, 1 + steps):
                for f in range(2 * parts):
                    S[state, f, x, pl.ds(first, 8), :] = zero_rows
            return carry

        lax.fori_loop(EDGE, EDGE + size_x, body, 0)

    pl.when(px == 0)(lambda: zero_planes(0))
    pl.when(px == n_px - 1)(lambda: zero_planes(EDGE + size_x))
    pl.when(py == 0)(lambda: zero_strip(0))
    pl.when(py == n_py - 1)(lambda: zero_strip(TOP + size_y))

    def halo_copies(ref, lead, group):
        def at(x, y):
            return ref.at[lead + (x, y)]

        x_all, y_all = cells
        last_x, last_y = EDGE + size_x, TOP + size_y
        moves = (
            ("px", 1, at(pl.ds(last_x - EDGE, EDGE), y_all), at(pl.ds(0, EDGE), y_all)),
            ("px", -1, at(pl.ds(EDGE, EDGE), y_all), at(pl.ds(last_x, EDGE), y_all)),
            ("py", 1, at(x_all, pl.ds(last_y - EDGE, EDGE)), at(x_all, pl.ds(TOP - EDGE, EDGE))),
            ("py", -1, at(x_all, pl.ds(TOP, EDGE)), at(x_all, pl.ds(last_y, EDGE))),
        )
        copies = []
        for way, (axis, k, src, dst) in enumerate(moves):
            copies.append(
                pltpu.make_async_remote_copy(
                    src,
                    dst,
                    halo_send.at[group, way],
                    halo_recv.at[group, way],
                    device_id={axis: peer(axis, k + count[axis])},
                    device_id_type=MESH,
                )
            )
        can_send = (px < n_px - 1, px > 0, py < n_py - 1, py > 0)
        can_recv = (px > 0, px < n_px - 1, py > 0, py < n_py - 1)
        return copies, can_send, can_recv

    def send_halo(halo):
        copies, can_send, _ = halo
        for way in (2, 3, 0, 1):
            pl.when(can_send[way])(copies[way].start)

    def wait_halo(halo):
        copies, can_send, can_recv = halo
        for way in range(4):
            pl.when(can_send[way])(copies[way].wait_send)
            pl.when(can_recv[way])(copies[way].wait_recv)

    halo_b = halo_copies(bpad, (), 0)
    halo_w = {
        (state, kind): halo_copies(S, (state, pl.ds(kind * parts, parts)), 2 * state - 1 + kind)
        for state in range(1, 1 + steps)
        for kind in range(2)
    }

    def column_copies(values, cols, lane):
        return [
            pltpu.make_async_remote_copy(
                values.at[:, pl.ds(peer("dom", k) * share, share)],
                cols.at[pl.ds(dom * parts, parts)],
                col_send.at[lane, k],
                col_recv.at[lane, k],
                device_id={"dom": peer("dom", k)},
                device_id_type=MESH,
            )
            for k in range(1, n_dom)
        ]

    def own_column(values, cols, lane):
        return pltpu.make_async_copy(
            values.at[:, pl.ds(dom * share, share)], cols.at[pl.ds(dom * parts, parts)], col_send.at[lane, 0]
        )

    slots = []
    for _ in range(2):
        for axis in ("px", "py", "dom"):
            slots.append(axis)

    def sum_copies(buffer, axis, slot):
        return [
            pltpu.make_async_remote_copy(
                buffer.at[coord[axis]],
                buffer.at[coord[axis]],
                sum_send.at[slot, k],
                sum_recv.at[slot, k],
                device_id={axis: peer(axis, k)},
                device_id_type=MESH,
            )
            for k in range(1, count[axis])
        ]

    def sum_send_off(buffer, axis, slot, value):
        buffer[coord[axis]] = value
        for copy in sum_copies(buffer, axis, slot):
            copy.start()

    def sum_gather(buffer, axis, slot):
        for copy in sum_copies(buffer, axis, slot):
            copy.wait()
        value = buffer[0]
        for k in range(1, count[axis]):
            value = value + buffer[k]
        return value

    def wave_step(step, kind):
        now, before, later = step + 1, step, step + 2
        last = step == steps - 1

        def plane(x, carry):
            sums = list(carry)
            for t in range(tiles):
                rows = pl.ds(8 * t, 8)
                weights = [C[k, x, rows, :] for k in range(19)]
                fade = damp[x, rows, :]
                for p in range(parts):
                    f = kind * parts + p
                    here = S[now, f, x + EDGE, pl.ds(TOP + 8 * t, 8), :]
                    along_x = [S[now, f, x + EDGE + k, pl.ds(TOP + 8 * t, 8), :] for k in SHIFTS]
                    along_y = [S[now, f, x + EDGE, pl.ds(TOP + 8 * t + k, 8), :] for k in SHIFTS]
                    along_z = [pltpu.roll(here, (size_z - k) % size_z, 1) for k in SHIFTS]
                    terms = [weights[0] * here]
                    for base, values in ((1, along_x), (7, along_y), (13, along_z)):
                        part = None
                        for k, value in enumerate(values):
                            term = weights[base + k] * value
                            part = term if part is None else part + term
                        terms.append(part)
                    lap = (terms[0] + terms[1]) + (terms[2] + terms[3])
                    speed = vel[p, x, rows, :]
                    old = S[before, f, x + EDGE, pl.ds(TOP + 8 * t, 8), :]
                    bend = old - 2.0 * here
                    new = (speed * speed) * lap - bend
                    if kind == 0:
                        new = new + src_hot[p, x, rows, :] * (STEP_SQ * wavelet[p, step])
                    else:
                        new = new + inj[step, p, pl.ds(pl.multiple_of(x * size_y, size_y) + 8 * t, 8), :]
                    new = fade * new
                    S[later, f, x + EDGE, pl.ds(TOP + 8 * t, 8), :] = new
                    if kind == 0:
                        other = S[now, parts + p, x + EDGE, pl.ds(TOP + 8 * t, 8), :]
                        add = other * (new + bend)
                        if step > 0:
                            add = add + grad[p, x, rows, :]
                        if last:
                            add = add * (-2.0 / (speed * speed * speed))
                            sums[p] = sums[p] + add * add
                        grad[p, x, rows, :] = add
            return tuple(sums)

        start = tuple(jnp.zeros((8, size_z), F32) for _ in range(parts)) if kind == 0 and last else ()
        return lax.fori_loop(0, size_x, plane, start)

    for copy in loads[:4]:
        copy.wait()
    pl.semaphore_wait(barrier, (n_px - 1) + (n_py - 1) + (n_dom - 1))
    send_halo(halo_b)
    send_halo(halo_w[1, 0])
    send_halo(halo_w[1, 1])
    model_moves = column_copies(vel, mcols, 0)
    for copy in model_moves:
        copy.start()
    model_own = own_column(vel, mcols, 0)
    model_own.start()

    widths = [sponge[k].astype(F32) for k in range(6)]
    base_x, base_y = px * size_x, py * size_y
    fade_yz = [
        sponge_part((row8 + (8 * t + base_y)).astype(F32), float(total_y), widths[2], widths[3])
        + sponge_part(lane8.astype(F32), float(size_z), widths[4], widths[5])
        for t in range(tiles)
    ]

    def tables(x, carry):
        at_x = jnp.full((8, size_z), x + base_x, jnp.int32)
        fade_x = sponge_part(at_x.astype(F32), float(total_x), widths[0], widths[1])
        for t in range(tiles):
            rows = pl.ds(8 * t, 8)
            damp[x, rows, :] = jnp.exp(-(fade_x + fade_yz[t]))
            flat = (at_x * total_y + (row8 + (8 * t + base_y))) * size_z + lane8
            for p in range(parts):
                src_hot[p, x, rows, :] = jnp.where(flat == sources[p], 1.0, 0.0)
        return carry

    lax.fori_loop(0, size_x, tables, 0)

    z_bits, y_bits = size_z.bit_length() - 1, total_y.bit_length() - 1
    n_recv = receivers.shape[1]
    for p in range(parts):
        index = receivers[pl.ds(p, 1), :]
        local_x = (index >> (z_bits + y_bits)) - base_x
        local_y = ((index >> z_bits) & (total_y - 1)) - base_y
        depth = index & (size_z - 1)
        inside = (local_x >= 0) & (local_x < size_x) & (local_y >= 0) & (local_y < size_y)
        at_plane = jnp.where(inside, local_x * size_y + local_y, -1)
        hit = lax.broadcasted_iota(jnp.int32, (size_z, n_recv), 0) == depth
        for s in range(steps):
            amount = STEP_SQ * misfit[p, pl.ds(s, 1), :]
            high = amount.astype(BF16).astype(F32)
            b_hi[s] = jnp.where(hit, high, 0.0).astype(BF16)
            b_lo[s] = jnp.where(hit, amount - high, 0.0).astype(BF16)

        def spread_rows(m, carry):
            rows = lax.broadcasted_iota(jnp.int32, (128, n_recv), 0) + m * 128
            hot = jnp.where(rows == at_plane, 1.0, 0.0).astype(BF16)
            for s in range(steps):
                inj[s, p, pl.ds(pl.multiple_of(m * 128, 128), 128), :] = lax.dot_general(
                    hot, b_hi[s], NT, preferred_element_type=F32
                ) + lax.dot_general(hot, b_lo[s], NT, preferred_element_type=F32)
            return carry

        lax.fori_loop(0, size_x * size_y // 128, spread_rows, 0)

    wait_halo(halo_b)

    def stencil(x, carry):
        for t in range(tiles):
            rows = pl.ds(8 * t, 8)
            here = bpad[x + EDGE, pl.ds(TOP + 8 * t, 8), :]
            scale = (0.5 * STEP_SQ) / here
            center = None
            for base, axis in ((1, 0), (7, 1), (13, 2)):
                around = {0: here}
                for k in (-2, -1, 1, 2):
                    if axis == 0:
                        around[k] = bpad[x + EDGE + k, pl.ds(TOP + 8 * t, 8), :]
                    elif axis == 1:
                        around[k] = bpad[x + EDGE, pl.ds(TOP + 8 * t + k, 8), :]
                    else:
                        inside = (lane8 + k >= 0) & (lane8 + k < size_z)
                        around[k] = jnp.where(inside, pltpu.roll(here, (size_z - k) % size_z, 1), 0.0)
                faces = [scale * (around[k] + around[k + 1]) for k in (-2, -1, 0, 1)]
                weights = axis_coefs(faces)
                center = weights[0] if center is None else center + weights[0]
                for at, (k, weight) in enumerate(zip(SHIFTS, weights[1:])):
                    if axis == 2:
                        inside = (lane8 + k >= 0) & (lane8 + k < size_z)
                        weight = jnp.where(inside, weight, 0.0)
                    C[base + at, x, rows, :] = weight
            C[0, x, rows, :] = center
        return carry

    lax.fori_loop(0, size_x, stencil, 0)

    for copy in loads[4:]:
        copy.wait()
    grad_sums = None
    for step in range(steps - 1):
        for kind in range(2):
            wait_halo(halo_w[step + 1, kind])
            wave_step(step, kind)
            send_halo(halo_w[step + 2, kind])

    model_own.wait()
    for copy in model_moves:
        copy.wait()
    blocks = [(a, pl.ds(8 * t, 8)) for a in range(share) for t in range(tiles)]

    def distances(i, carry):
        mine = [mcols[i, a, rows, :] for a, rows in blocks]
        for j in range(particles):
            total = None
            for value, (a, rows) in zip(mine, blocks):
                gap = value - mcols[j, a, rows, :]
                total = gap * gap if total is None else total + gap * gap
            T[i, pl.ds(j, 1), :] = jnp.sum(total, axis=0, keepdims=True)
        return carry

    lax.fori_loop(0, particles, distances, 0)
    pairs = particles * particles
    lane_sums = lax.dot_general(
        jnp.ones((8, size_z), F32),
        T[...].reshape(pairs, size_z),
        NT,
        precision=HIGHEST,
        preferred_element_type=F32,
    )
    gram = jnp.where(row8 == 0, lane_sums[:, :128], lane_sums[:, 128:])
    sum_send_off(gram_dom, "dom", 2, gram)

    step = steps - 1
    wait_halo(halo_w[step + 1, 0])
    grad_sums = wave_step(step, 0)
    grad_moves = column_copies(grad, gcols, 1)
    for copy in grad_moves:
        copy.start()
    grad_own = own_column(grad, gcols, 1)
    grad_own.start()
    norm = jnp.zeros((8, size_z), F32)
    for p in range(parts):
        norm = jnp.where(lane8 % particles == dom * parts + p, jnp.sum(grad_sums[p]), norm)
    sum_send_off(norm_px, "px", 3, norm)
    gram = sum_gather(gram_dom, "dom", 2)
    sum_send_off(gram_px, "px", 0, gram)
    norm = sum_gather(norm_px, "px", 3)
    sum_send_off(norm_py, "py", 4, norm)
    gram = sum_gather(gram_px, "px", 0)
    sum_send_off(gram_py, "py", 1, gram)

    wait_halo(halo_w[step + 1, 1])
    wave_step(step, 1)
    outs = [
        pltpu.make_async_copy(S.at[(state, pl.ds(kind * parts, parts)) + cells], out, out_sem.at[at])
        for at, (state, kind, out) in enumerate(
            ((steps, 0, fb_out), (steps + 1, 0, fa_out), (steps, 1, ab_out), (steps + 1, 1, aa_out))
        )
    ]
    for copy in outs:
        copy.start()
    norm = sum_gather(norm_py, "py", 4)
    sum_send_off(norm_dom, "dom", 5, norm)
    gram = sum_gather(gram_py, "py", 1)

    width = jnp.sum(jnp.where(row8 < 2, gram, 0.0)) / (particles * (particles - 1)) + EPSILON
    weight = jnp.exp(-gram / width)
    square = lax.broadcasted_iota(jnp.int32, (128, 128), 0) == lax.broadcasted_iota(jnp.int32, (128, 128), 1)

    def spread_out_rows(lane, tile):
        for half in range(pairs // 128):
            diagonal = jnp.where(square, tile[half : half + 1, :], 0.0)
            block = jnp.dot(diagonal, jnp.ones((128, size_z), F32), precision=HIGHEST, preferred_element_type=F32)
            KB[lane, pl.ds(half * 128 // particles, 128 // particles)] = block.reshape(
                128 // particles, particles, size_z
            )

    def back_copy(mixed, out, lane, k, target):
        return pltpu.make_async_remote_copy(
            mixed.at[pl.ds(target * parts, parts)],
            out.at[:, pl.ds(dom * share, share)],
            col_send.at[lane, k],
            col_recv.at[lane, k],
            device_id={"dom": target},
            device_id_type=MESH,
        )

    def mix(cols, lane, mixed, out, sem_lane, model):
        def one(k, carry):
            target = lax.rem(dom + k, n_dom)
            for p in range(parts):
                i = target * parts + p
                factors = [KB[lane, i, pl.ds(j, 1), :] for j in range(particles)]
                if model:
                    row_sum = factors[0]
                    for factor in factors[1:]:
                        row_sum = row_sum + factor
                for a, rows in blocks:
                    total = None
                    for j in range(particles):
                        term = factors[j] * cols[j, a, rows, :]
                        total = term if total is None else total + term
                    if model:
                        total = cols[i, a, rows, :] * row_sum - total
                    mixed[i, a, rows, :] = total
            pl.when(k < n_dom)(lambda: back_copy(mixed, out, sem_lane, lax.rem(k, n_dom), target).start())
            return carry

        lax.fori_loop(1, n_dom + 1, one, 0)
        own = pltpu.make_async_copy(
            mixed.at[pl.ds(dom * parts, parts)], out.at[:, pl.ds(dom * share, share)], col_send.at[sem_lane, 0]
        )
        own.start()
        return own

    spread_out_rows(0, weight)
    spread_own = mix(mcols, 0, mix_m, spread_out, 2, True)

    norm = sum_gather(norm_dom, "dom", 5)
    scale = 1.0 / jnp.sqrt(norm / float(total_x * total_y * size_z) + EPSILON)
    spread_out_rows(1, weight * scale)
    grad_own.wait()
    for copy in grad_moves:
        copy.wait()
    drift_own = mix(gcols, 1, mix_g, drift_out, 3, False)

    for copy in outs:
        copy.wait()
    spread_own.wait()
    drift_own.wait()
    for k in range(1, n_dom):
        back_copy(mix_m, spread_out, 2, k, peer("dom", k)).wait()
    for k in range(1, n_dom):
        back_copy(mix_g, drift_out, 3, k, peer("dom", k)).wait()


def on_device(counts, *args):
    velocity, wavelet, receivers = args[0], args[7], args[8]
    parts, size_x, size_y, size_z = velocity.shape
    steps, n_recv = wavelet.shape[1], receivers.shape[1]
    n_px, n_py, n_dom = counts
    particles = parts * n_dom
    share = size_x // n_dom
    pad_x, pad_y = size_x + 2 * EDGE, size_y + 2 * TOP
    whole = (parts, size_x, size_y, size_z)
    cols = (particles, share, size_y, size_z)
    most = max(counts)
    anywhere = pl.BlockSpec(memory_space=pl.ANY)
    vmem = pl.BlockSpec(memory_space=pltpu.VMEM)
    smem = pl.BlockSpec(memory_space=pltpu.SMEM)
    dma = pltpu.SemaphoreType.DMA
    return pl.pallas_call(
        functools.partial(kernel, counts),
        out_shape=[jax.ShapeDtypeStruct(whole, F32)] * 6,
        in_specs=[anywhere] * 6 + [smem, smem, vmem, vmem, smem],
        out_specs=[anywhere] * 6,
        scratch_shapes=[
            pltpu.VMEM((steps + 2, 2 * parts, pad_x, pad_y, size_z), F32),
            pltpu.VMEM(whole, F32),
            pltpu.VMEM((pad_x, pad_y, size_z), F32),
            pltpu.VMEM((19, size_x, size_y, size_z), F32),
            pltpu.VMEM((size_x, size_y, size_z), F32),
            pltpu.VMEM(whole, F32),
            pltpu.VMEM((steps, parts, size_x * size_y, size_z), F32),
            pltpu.VMEM((steps, size_z, n_recv), BF16),
            pltpu.VMEM((steps, size_z, n_recv), BF16),
            pltpu.VMEM(whole, F32),
            pltpu.VMEM(cols, F32),
            pltpu.VMEM(cols, F32),
            pltpu.VMEM(cols, F32),
            pltpu.VMEM(cols, F32),
            pltpu.VMEM((particles, particles, size_z), F32),
            pltpu.VMEM((2, particles, particles, size_z), F32),
            pltpu.VMEM((n_px, 8, size_z), F32),
            pltpu.VMEM((n_py, 8, size_z), F32),
            pltpu.VMEM((n_dom, 8, size_z), F32),
            pltpu.VMEM((n_px, 8, size_z), F32),
            pltpu.VMEM((n_py, 8, size_z), F32),
            pltpu.VMEM((n_dom, 8, size_z), F32),
            dma((6,)),
            dma((1 + 2 * steps, 4)),
            dma((1 + 2 * steps, 4)),
            dma((4, n_dom)),
            dma((4, n_dom)),
            dma((6, most)),
            dma((6, most)),
            dma((4,)),
        ],
        compiler_params=pltpu.CompilerParams(collective_id=0, has_side_effects=True, vmem_limit_bytes=60 * 1024 * 1024),
    )(*args)


def solution(mesh):
    counts = (mesh.shape["px"], mesh.shape["py"], mesh.shape["dom"])
    field = P("dom", "px", "py", None)
    return jax.shard_map(
        functools.partial(on_device, counts),
        mesh=mesh,
        in_specs=(
            field,
            P("px", "py", None),
            field,
            field,
            field,
            field,
            P("dom"),
            P("dom", None),
            P("dom", None),
            P("dom", None, None),
            P(),
        ),
        out_specs=(field,) * 6,
        check_vma=False,
    )
```

```python
import functools

import jax
import jax.numpy as jnp
from jax import lax
from jax.experimental import pallas as pl
from jax.experimental.pallas import tpu as pltpu
from jax.sharding import PartitionSpec as P

EPSILON = 1e-06
TIME_STEP = 0.18
STEP_SQ = TIME_STEP * TIME_STEP
SPONGE_RATE = 0.5
NEAR = 9.0 / 8.0
FAR = 1.0 / 24.0
MESH = pl.DeviceIdType.MESH
F32 = jnp.float32
BF16 = jnp.bfloat16
HIGHEST = lax.Precision.HIGHEST
NT = (((1,), (1,)), ((), ()))
EDGE = 3
TOP = 8


def sponge_part(position, length, low, high):
    far_side = (length - 1) - position
    low_part = jnp.where(position < low, jnp.square(SPONGE_RATE * (low - position) / low), 0.0)
    high_part = jnp.where(far_side < high, jnp.square(SPONGE_RATE * (high - far_side) / high), 0.0)
    return low_part + high_part


def axis_coefs(faces):
    below2, below, here, above = faces
    near_sq, cross, far_sq = NEAR * NEAR, NEAR * FAR, FAR * FAR
    return (
        -near_sq * (here + below) - far_sq * (above + below2),
        near_sq * here + cross * (below + above),
        near_sq * below + cross * (here + below2),
        -cross * (here + above),
        -cross * (below + below2),
        far_sq * above,
        far_sq * below2,
    )


SHIFTS = (1, -1, 2, -2, 3, -3)


def kernel(
    counts,
    vel_in,
    buoy_in,
    fp_in,
    fn_in,
    ap_in,
    an_in,
    sources,
    wavelet,
    receivers,
    misfit,
    sponge,
    fb_out,
    fa_out,
    ab_out,
    aa_out,
    drift_out,
    spread_out,
    S,
    vel,
    bpad,
    C,
    damp,
    src_hot,
    inj,
    b_parts,
    hot,
    fade_speed,
    grad_scale,
    base,
    grad,
    mcols,
    gcols,
    mix_m,
    mix_g,
    T,
    KB,
    gram_px,
    gram_py,
    gram_dom,
    norm_px,
    norm_py,
    norm_dom,
    load_sem,
    halo_send,
    halo_recv,
    col_send,
    col_recv,
    sum_send,
    sum_recv,
):
    n_px, n_py, n_dom = counts
    parts, size_x, size_y, size_z = vel.shape
    steps = wavelet.shape[1]
    tiles = size_y // 8
    px, py, dom = lax.axis_index("px"), lax.axis_index("py"), lax.axis_index("dom")
    coord = {"px": px, "py": py, "dom": dom}
    count = {"px": n_px, "py": n_py, "dom": n_dom}
    total_x, total_y = size_x * n_px, size_y * n_py
    particles = parts * n_dom
    share = size_x // n_dom
    cells = pl.ds(EDGE, size_x), pl.ds(TOP, size_y)
    row8 = lax.broadcasted_iota(jnp.int32, (8, size_z), 0)
    lane8 = lax.broadcasted_iota(jnp.int32, (8, size_z), 1)

    def peer(axis, k):
        return lax.rem(coord[axis] + k, count[axis])

    barrier = pltpu.get_barrier_semaphore()
    for axis in ("px", "py", "dom"):
        for k in range(1, count[axis]):
            pl.semaphore_signal(barrier, inc=1, device_id={axis: peer(axis, k)}, device_id_type=MESH)

    loads = [
        pltpu.make_async_copy(vel_in, vel, load_sem.at[0]),
        pltpu.make_async_copy(buoy_in, bpad.at[cells], load_sem.at[1]),
        pltpu.make_async_copy(fn_in, S.at[(1, pl.ds(0, parts)) + cells], load_sem.at[2]),
        pltpu.make_async_copy(an_in, S.at[(1, pl.ds(parts, parts)) + cells], load_sem.at[3]),
        pltpu.make_async_copy(fp_in, S.at[(0, pl.ds(0, parts)) + cells], load_sem.at[4]),
        pltpu.make_async_copy(ap_in, S.at[(0, pl.ds(parts, parts)) + cells], load_sem.at[5]),
    ]
    for copy in loads:
        copy.start()

    zero_rows = jnp.zeros((8, size_z), F32)
    zero_plane = jnp.zeros((size_y, size_z), F32)

    def zero_planes(first):
        for k in range(EDGE):
            bpad[first + k, pl.ds(TOP, size_y), :] = zero_plane
            for state in range(1, 1 + steps):
                for f in range(2 * parts):
                    S[state, f, first + k, pl.ds(TOP, size_y), :] = zero_plane

    def zero_strip(first):
        def body(x, carry):
            bpad[x, pl.ds(first, 8), :] = zero_rows
            for state in range(1, 1 + steps):
                for f in range(2 * parts):
                    S[state, f, x, pl.ds(first, 8), :] = zero_rows
            return carry

        lax.fori_loop(EDGE, EDGE + size_x, body, 0)

    pl.when(px == 0)(lambda: zero_planes(0))
    pl.when(px == n_px - 1)(lambda: zero_planes(EDGE + size_x))
    pl.when(py == 0)(lambda: zero_strip(0))
    pl.when(py == n_py - 1)(lambda: zero_strip(TOP + size_y))

    def halo_copies(ref, lead, group):
        def at(x, y):
            return ref.at[lead + (x, y)]

        x_all, y_all = cells
        last_x, last_y = EDGE + size_x, TOP + size_y
        moves = (
            ("px", 1, at(pl.ds(last_x - EDGE, EDGE), y_all), at(pl.ds(0, EDGE), y_all)),
            ("px", -1, at(pl.ds(EDGE, EDGE), y_all), at(pl.ds(last_x, EDGE), y_all)),
            ("py", 1, at(x_all, pl.ds(last_y - EDGE, EDGE)), at(x_all, pl.ds(TOP - EDGE, EDGE))),
            ("py", -1, at(x_all, pl.ds(TOP, EDGE)), at(x_all, pl.ds(last_y, EDGE))),
        )
        copies = []
        for way, (axis, k, src, dst) in enumerate(moves):
            copies.append(
                pltpu.make_async_remote_copy(
                    src,
                    dst,
                    halo_send.at[group, way],
                    halo_recv.at[group, way],
                    device_id={axis: peer(axis, k + count[axis])},
                    device_id_type=MESH,
                )
            )
        can_send = (px < n_px - 1, px > 0, py < n_py - 1, py > 0)
        can_recv = (px > 0, px < n_px - 1, py > 0, py < n_py - 1)
        return copies, can_send, can_recv

    def send_halo(halo):
        copies, can_send, _ = halo
        for way in (2, 3, 0, 1):
            pl.when(can_send[way])(copies[way].start)

    def wait_halo(halo):
        copies, can_send, can_recv = halo
        for way in range(4):
            pl.when(can_send[way])(copies[way].wait_send)
            pl.when(can_recv[way])(copies[way].wait_recv)

    halo_b = halo_copies(bpad, (), 0)
    halo_w = {
        (state, kind): halo_copies(S, (state, pl.ds(kind * parts, parts)), 2 * state - 1 + kind)
        for state in range(1, 1 + steps)
        for kind in range(2)
    }

    def column_copies(values, cols, lane):
        return [
            pltpu.make_async_remote_copy(
                values.at[:, pl.ds(peer("dom", k) * share, share)],
                cols.at[pl.ds(dom * parts, parts)],
                col_send.at[lane, k],
                col_recv.at[lane, k],
                device_id={"dom": peer("dom", k)},
                device_id_type=MESH,
            )
            for k in range(1, n_dom)
        ]

    def own_column(values, cols, lane):
        return pltpu.make_async_copy(
            values.at[:, pl.ds(dom * share, share)], cols.at[pl.ds(dom * parts, parts)], col_send.at[lane, 0]
        )

    slots = []
    for _ in range(2):
        for axis in ("px", "py", "dom"):
            slots.append(axis)

    def sum_copies(buffer, axis, slot):
        return [
            pltpu.make_async_remote_copy(
                buffer.at[coord[axis]],
                buffer.at[coord[axis]],
                sum_send.at[slot, k],
                sum_recv.at[slot, k],
                device_id={axis: peer(axis, k)},
                device_id_type=MESH,
            )
            for k in range(1, count[axis])
        ]

    def sum_send_off(buffer, axis, slot, value):
        buffer[coord[axis]] = value
        for copy in sum_copies(buffer, axis, slot):
            copy.start()

    def sum_gather(buffer, axis, slot):
        for copy in sum_copies(buffer, axis, slot):
            copy.wait()
        value = buffer[0]
        for k in range(1, count[axis]):
            value = value + buffer[k]
        return value

    def pre_step(step, kind):
        now, before = step + 1, step

        def plane(x, carry):
            for t in range(tiles):
                rows, wide = pl.ds(8 * t, 8), pl.ds(TOP + 8 * t, 8)
                weights = [C[k, x, rows, :] for k in (0, 13, 14, 15, 16, 17, 18)]
                fade = damp[x, rows, :]
                for p in range(parts):
                    f = kind * parts + p
                    here = S[now, f, x + EDGE, wide, :]
                    old = S[before, f, x + EDGE, wide, :]
                    lap = weights[0] * here
                    for k, weight in zip(SHIFTS, weights[1:]):
                        lap = lap + weight * pltpu.roll(here, (size_z - k) % size_z, 1)
                    if kind == 0:
                        add = src_hot[p, x, rows, :] * (STEP_SQ * wavelet[p, step])
                    else:
                        add = inj[step, p, pl.ds(pl.multiple_of(x * size_y, size_y) + 8 * t, 8), :]
                    base[kind, p, x, rows, :] = fade_speed[p, x, rows, :] * lap + fade * ((here + here) - old + add)
                    if kind == 0 and step > 0:
                        older = S[before - 1, f, x + EDGE, wide, :]
                        part = S[before, parts + p, x + EDGE, wide, :] * ((here - (old + old)) + older)
                        if step > 1:
                            part = part + grad[p, x, rows, :]
                        grad[p, x, rows, :] = part
            return carry

        lax.fori_loop(0, size_x, plane, 0, unroll=2)

    def post_step(step, kind):
        now, before, later = step + 1, step, step + 2
        last = step == steps - 1

        def plane(x, carry):
            sums = list(carry)
            for t in range(tiles):
                rows, wide = pl.ds(8 * t, 8), pl.ds(TOP + 8 * t, 8)
                weights = [C[1 + k, x, rows, :] for k in range(12)]
                for p in range(parts):
                    f = kind * parts + p
                    lap = None
                    for k, weight in zip(SHIFTS, weights[:6]):
                        term = weight * S[now, f, x + EDGE + k, wide, :]
                        lap = term if lap is None else lap + term
                    for k, weight in zip(SHIFTS, weights[6:]):
                        lap = lap + weight * S[now, f, x + EDGE, pl.ds(TOP + 8 * t + k, 8), :]
                    new = base[kind, p, x, rows, :] + fade_speed[p, x, rows, :] * lap
                    if not last:
                        S[later, f, x + EDGE, wide, :] = new
                    if step >= steps - 2:
                        results[kind][step - steps + 2][p, x, rows, :] = new
                    if kind == 0 and last:
                        here = S[now, f, x + EDGE, wide, :]
                        bend = (new - (here + here)) + S[before, f, x + EDGE, wide, :]
                        part = S[now, parts + p, x + EDGE, wide, :] * bend
                        if step > 0:
                            part = part + grad[p, x, rows, :]
                        part = part * grad_scale[p, x, rows, :]
                        sums[p] = sums[p] + part * part
                        grad[p, x, rows, :] = part
            return tuple(sums)

        start = tuple(jnp.zeros((8, size_z), F32) for _ in range(parts)) if kind == 0 and last else ()
        return lax.fori_loop(0, size_x, plane, start, unroll=2)

    results = ((fb_out, fa_out), (ab_out, aa_out))

    for copy in loads[:4]:
        copy.wait()
    pl.semaphore_wait(barrier, (n_px - 1) + (n_py - 1) + (n_dom - 1))
    send_halo(halo_b)
    send_halo(halo_w[1, 0])
    send_halo(halo_w[1, 1])
    model_moves = column_copies(vel, mcols, 0)
    for copy in model_moves:
        copy.start()
    model_own = own_column(vel, mcols, 0)
    model_own.start()

    widths = [sponge[k].astype(F32) for k in range(6)]
    base_x, base_y = px * size_x, py * size_y
    fade_yz = [
        sponge_part((row8 + (8 * t + base_y)).astype(F32), float(total_y), widths[2], widths[3])
        + sponge_part(lane8.astype(F32), float(size_z), widths[4], widths[5])
        for t in range(tiles)
    ]

    def tables(x, carry):
        at_x = jnp.full((8, size_z), x + base_x, jnp.int32)
        fade_x = sponge_part(at_x.astype(F32), float(total_x), widths[0], widths[1])
        for t in range(tiles):
            rows = pl.ds(8 * t, 8)
            damp[x, rows, :] = jnp.exp(-(fade_x + fade_yz[t]))
            flat = (at_x * total_y + (row8 + (8 * t + base_y))) * size_z + lane8
            for p in range(parts):
                speed = vel[p, x, rows, :]
                square = speed * speed
                fade_speed[p, x, rows, :] = damp[x, rows, :] * square
                grad_scale[p, x, rows, :] = -2.0 / (square * speed)
                src_hot[p, x, rows, :] = jnp.where(flat == sources[p], 1.0, 0.0)
        return carry

    lax.fori_loop(0, size_x, tables, 0)

    z_bits, y_bits = size_z.bit_length() - 1, total_y.bit_length() - 1
    n_recv = receivers.shape[1]
    row16 = lax.broadcasted_iota(jnp.int32, (16, n_recv), 0)

    def inject(p):
        index = receivers[pl.ds(p, 1), :]
        local_x = (index >> (z_bits + y_bits)) - base_x
        local_y = ((index >> z_bits) & (total_y - 1)) - base_y
        inside = (local_x >= 0) & (local_x < size_x) & (local_y >= 0) & (local_y < size_y)
        at_plane = jnp.where(inside, local_x * size_y + local_y, -1) - row16
        depth = (index & (size_z - 1)) - row16
        amounts = []
        for s in range(steps):
            amount = STEP_SQ * misfit[s, pl.ds(p, 1), :]
            high = amount.astype(BF16).astype(F32)
            amounts += [high, amount - high]

        def depths(m, carry):
            hit = depth == m * 16
            for k, amount in enumerate(amounts):
                b_parts[k, pl.ds(pl.multiple_of(m * 16, 16), 16), :] = jnp.where(hit, amount, 0.0).astype(BF16)
            return carry

        lax.fori_loop(0, size_z // 16, depths, 0)

        def planes(m, carry):
            hot[pl.ds(pl.multiple_of(m * 16, 16), 16), :] = jnp.where(at_plane == m * 16, 1.0, 0.0).astype(BF16)
            return carry

        lax.fori_loop(0, size_x * size_y // 16, planes, 0, unroll=2)
        for s in range(steps):
            both = lax.dot_general(
                hot[...],
                b_parts[pl.ds(2 * s, 2)].reshape(2 * size_z, n_recv),
                NT,
                preferred_element_type=F32,
            )
            inj[s, p] = both[:, :size_z] + both[:, size_z:]

    inject(0)

    wait_halo(halo_b)

    def stencil(x, carry):
        for t in range(tiles):
            rows = pl.ds(8 * t, 8)
            here = bpad[x + EDGE, pl.ds(TOP + 8 * t, 8), :]
            scale = (0.5 * STEP_SQ) / here
            center = None
            for base, axis in ((1, 0), (7, 1), (13, 2)):
                around = {0: here}
                for k in (-2, -1, 1, 2):
                    if axis == 0:
                        around[k] = bpad[x + EDGE + k, pl.ds(TOP + 8 * t, 8), :]
                    elif axis == 1:
                        around[k] = bpad[x + EDGE, pl.ds(TOP + 8 * t + k, 8), :]
                    else:
                        inside = (lane8 + k >= 0) & (lane8 + k < size_z)
                        around[k] = jnp.where(inside, pltpu.roll(here, (size_z - k) % size_z, 1), 0.0)
                faces = [scale * (around[k] + around[k + 1]) for k in (-2, -1, 0, 1)]
                weights = axis_coefs(faces)
                center = weights[0] if center is None else center + weights[0]
                for at, (k, weight) in enumerate(zip(SHIFTS, weights[1:])):
                    if axis == 2:
                        inside = (lane8 + k >= 0) & (lane8 + k < size_z)
                        weight = jnp.where(inside, weight, 0.0)
                    C[base + at, x, rows, :] = weight
            C[0, x, rows, :] = center
        return carry

    lax.fori_loop(0, size_x, stencil, 0)

    for copy in loads[4:]:
        copy.wait()
    pre_step(0, 0)
    wait_halo(halo_w[1, 0])
    post_step(0, 0)
    send_halo(halo_w[2, 0])
    for p in range(1, parts):
        inject(p)
    pre_step(0, 1)
    wait_halo(halo_w[1, 1])
    post_step(0, 1)
    send_halo(halo_w[2, 1])
    pre_step(1, 0)
    wait_halo(halo_w[2, 0])
    post_step(1, 0)
    send_halo(halo_w[3, 0])
    pre_step(2, 0)

    model_own.wait()
    for copy in model_moves:
        copy.wait()
    blocks = [(a, pl.ds(8 * t, 8)) for a in range(share) for t in range(tiles)]

    def distances(i, carry):
        mine = [mcols[i, a, rows, :] for a, rows in blocks]
        for j in range(particles):
            total = None
            for value, (a, rows) in zip(mine, blocks):
                gap = value - mcols[j, a, rows, :]
                total = gap * gap if total is None else total + gap * gap
            T[i, pl.ds(j, 1), :] = jnp.sum(total, axis=0, keepdims=True)
        return carry

    lax.fori_loop(0, particles, distances, 0)
    pairs = particles * particles
    lane_sums = lax.dot_general(
        jnp.ones((8, size_z), F32),
        T[...].reshape(pairs, size_z),
        NT,
        precision=HIGHEST,
        preferred_element_type=F32,
    )
    gram = jnp.where(row8 == 0, lane_sums[:, :128], lane_sums[:, 128:])
    sum_send_off(gram_dom, "dom", 2, gram)
    pre_step(1, 1)
    wait_halo(halo_w[2, 1])
    post_step(1, 1)
    send_halo(halo_w[3, 1])

    wait_halo(halo_w[3, 0])
    grad_sums = post_step(2, 0)
    grad_moves = column_copies(grad, gcols, 1)
    for copy in grad_moves:
        copy.start()
    grad_own = own_column(grad, gcols, 1)
    grad_own.start()
    norm = jnp.zeros((8, size_z), F32)
    for p in range(parts):
        norm = jnp.where(lane8 % particles == dom * parts + p, jnp.sum(grad_sums[p]), norm)
    sum_send_off(norm_px, "px", 3, norm)
    gram = sum_gather(gram_dom, "dom", 2)
    sum_send_off(gram_px, "px", 0, gram)
    norm = sum_gather(norm_px, "px", 3)
    sum_send_off(norm_py, "py", 4, norm)
    gram = sum_gather(gram_px, "px", 0)
    sum_send_off(gram_py, "py", 1, gram)

    pre_step(2, 1)
    wait_halo(halo_w[3, 1])
    post_step(2, 1)
    norm = sum_gather(norm_py, "py", 4)
    sum_send_off(norm_dom, "dom", 5, norm)
    gram = sum_gather(gram_py, "py", 1)

    width = jnp.sum(jnp.where(row8 < 2, gram, 0.0)) / (particles * (particles - 1)) + EPSILON
    weight = jnp.exp(-gram / width)
    square = lax.broadcasted_iota(jnp.int32, (128, 128), 0) == lax.broadcasted_iota(jnp.int32, (128, 128), 1)

    def spread_out_rows(lane, tile):
        for half in range(pairs // 128):
            diagonal = jnp.where(square, tile[half : half + 1, :], 0.0)
            block = jnp.dot(diagonal, jnp.ones((128, size_z), F32), precision=HIGHEST, preferred_element_type=F32)
            KB[lane, pl.ds(half * 128 // particles, 128 // particles)] = block.reshape(
                128 // particles, particles, size_z
            )

    def back_copy(mixed, out, lane, k, target):
        return pltpu.make_async_remote_copy(
            mixed.at[pl.ds(target * parts, parts)],
            out.at[:, pl.ds(dom * share, share)],
            col_send.at[lane, k],
            col_recv.at[lane, k],
            device_id={"dom": target},
            device_id_type=MESH,
        )

    def mix(cols, lane, mixed, out, sem_lane, model):
        def one(k, carry):
            target = lax.rem(dom + k, n_dom)
            for p in range(parts):
                i = target * parts + p
                factors = [KB[lane, i, pl.ds(j, 1), :] for j in range(particles)]
                if model:
                    row_sum = factors[0]
                    for factor in factors[1:]:
                        row_sum = row_sum + factor
                for a, rows in blocks:
                    total = None
                    for j in range(particles):
                        term = factors[j] * cols[j, a, rows, :]
                        total = term if total is None else total + term
                    if model:
                        total = cols[i, a, rows, :] * row_sum - total
                    mixed[i, a, rows, :] = total
            pl.when(k < n_dom)(lambda: back_copy(mixed, out, sem_lane, lax.rem(k, n_dom), target).start())
            return carry

        lax.fori_loop(1, n_dom + 1, one, 0)
        own = pltpu.make_async_copy(
            mixed.at[pl.ds(dom * parts, parts)], out.at[:, pl.ds(dom * share, share)], col_send.at[sem_lane, 0]
        )
        own.start()
        return own

    spread_out_rows(0, weight)
    spread_own = mix(mcols, 0, mix_m, spread_out, 2, True)

    norm = sum_gather(norm_dom, "dom", 5)
    scale = 1.0 / jnp.sqrt(norm / float(total_x * total_y * size_z) + EPSILON)
    spread_out_rows(1, weight * scale)
    grad_own.wait()
    for copy in grad_moves:
        copy.wait()
    drift_own = mix(gcols, 1, mix_g, drift_out, 3, False)

    spread_own.wait()
    drift_own.wait()
    for k in range(1, n_dom):
        back_copy(mix_m, spread_out, 2, k, peer("dom", k)).wait()
    for k in range(1, n_dom):
        back_copy(mix_g, drift_out, 3, k, peer("dom", k)).wait()


def put_out(*refs):
    sem = refs[-1]
    copies = [pltpu.make_async_copy(refs[k], refs[6 + k], sem.at[k]) for k in range(6)]
    for copy in copies:
        copy.start()
    for copy in copies:
        copy.wait()


def on_device(counts, *args):
    velocity, wavelet, receivers = args[0], args[7], args[8]
    parts, size_x, size_y, size_z = velocity.shape
    steps, n_recv = wavelet.shape[1], receivers.shape[1]
    n_px, n_py, n_dom = counts
    particles = parts * n_dom
    share = size_x // n_dom
    pad_x, pad_y = size_x + 2 * EDGE, size_y + 2 * TOP
    whole = (parts, size_x, size_y, size_z)
    cols = (particles, share, size_y, size_z)
    most = max(counts)
    hbm = pl.BlockSpec(memory_space=pltpu.HBM)
    vmem = pl.BlockSpec(memory_space=pltpu.VMEM)
    smem = pl.BlockSpec(memory_space=pltpu.SMEM)
    dma = pltpu.SemaphoreType.DMA
    args = args[:9] + (jnp.transpose(args[9], (1, 0, 2)), args[10])
    results = pl.pallas_call(
        functools.partial(kernel, counts),
        out_shape=[pltpu.VMEM(whole, F32)] * 6,
        in_specs=[hbm] * 6 + [smem, smem, vmem, vmem, smem],
        out_specs=[vmem] * 6,
        scratch_shapes=[
            pltpu.VMEM((steps + 1, 2 * parts, pad_x, pad_y, size_z), F32),
            pltpu.VMEM(whole, F32),
            pltpu.VMEM((pad_x, pad_y, size_z), F32),
            pltpu.VMEM((19, size_x, size_y, size_z), F32),
            pltpu.VMEM((size_x, size_y, size_z), F32),
            pltpu.VMEM(whole, F32),
            pltpu.VMEM((steps, parts, size_x * size_y, size_z), F32),
            pltpu.VMEM((2 * steps, size_z, n_recv), BF16),
            pltpu.VMEM((size_x * size_y, n_recv), BF16),
            pltpu.VMEM(whole, F32),
            pltpu.VMEM(whole, F32),
            pltpu.VMEM((2,) + whole, F32),
            pltpu.VMEM(whole, F32),
            pltpu.VMEM(cols, F32),
            pltpu.VMEM(cols, F32),
            pltpu.VMEM(cols, F32),
            pltpu.VMEM(cols, F32),
            pltpu.VMEM((particles, particles, size_z), F32),
            pltpu.VMEM((2, particles, particles, size_z), F32),
            pltpu.VMEM((n_px, 8, size_z), F32),
            pltpu.VMEM((n_py, 8, size_z), F32),
            pltpu.VMEM((n_dom, 8, size_z), F32),
            pltpu.VMEM((n_px, 8, size_z), F32),
            pltpu.VMEM((n_py, 8, size_z), F32),
            pltpu.VMEM((n_dom, 8, size_z), F32),
            dma((6,)),
            dma((1 + 2 * steps, 4)),
            dma((1 + 2 * steps, 4)),
            dma((4, n_dom)),
            dma((4, n_dom)),
            dma((6, most)),
            dma((6, most)),
        ],
        compiler_params=pltpu.CompilerParams(collective_id=0, has_side_effects=True, vmem_limit_bytes=40 * 1024 * 1024),
    )(*[pltpu.with_memory_space_constraint(arg, pltpu.HBM) for arg in args])
    results = [pltpu.with_memory_space_constraint(result, pltpu.VMEM) for result in results]
    return pl.pallas_call(
        put_out,
        out_shape=[jax.ShapeDtypeStruct(whole, F32)] * 6,
        in_specs=[vmem] * 6,
        out_specs=[hbm] * 6,
        scratch_shapes=[dma((6,))],
    )(*results)


def solution(mesh):
    counts = (mesh.shape["px"], mesh.shape["py"], mesh.shape["dom"])
    field = P("dom", "px", "py", None)
    return jax.shard_map(
        functools.partial(on_device, counts),
        mesh=mesh,
        in_specs=(
            field,
            P("px", "py", None),
            field,
            field,
            field,
            field,
            P("dom"),
            P("dom", None),
            P("dom", None),
            P("dom", None, None),
            P(),
        ),
        out_specs=(field,) * 6,
        check_vma=False,
    )
```

```python
import functools

import jax
import jax.numpy as jnp
from jax import lax
from jax.experimental import pallas as pl
from jax.experimental.pallas import tpu as pltpu
from jax.sharding import PartitionSpec as P

EPSILON = 1e-06
TIME_STEP = 0.18
STEP_SQ = TIME_STEP * TIME_STEP
SPONGE_RATE = 0.5
NEAR = 9.0 / 8.0
FAR = 1.0 / 24.0
MESH = pl.DeviceIdType.MESH
F32 = jnp.float32
BF16 = jnp.bfloat16
HIGHEST = lax.Precision.HIGHEST
NT = (((1,), (1,)), ((), ()))
EDGE = 3
TOP = 8


def sponge_part(position, length, low, high):
    far_side = (length - 1) - position
    low_part = jnp.where(position < low, jnp.square(SPONGE_RATE * (low - position) / low), 0.0)
    high_part = jnp.where(far_side < high, jnp.square(SPONGE_RATE * (high - far_side) / high), 0.0)
    return low_part + high_part


def axis_coefs(faces):
    below2, below, here, above = faces
    near_sq, cross, far_sq = NEAR * NEAR, NEAR * FAR, FAR * FAR
    return (
        -near_sq * (here + below) - far_sq * (above + below2),
        near_sq * here + cross * (below + above),
        near_sq * below + cross * (here + below2),
        -cross * (here + above),
        -cross * (below + below2),
        far_sq * above,
        far_sq * below2,
    )


SHIFTS = (1, -1, 2, -2, 3, -3)


def kernel(
    counts,
    vel_in,
    buoy_in,
    fp_in,
    fn_in,
    ap_in,
    an_in,
    sources_in,
    wavelet_in,
    receivers_in,
    misfit_in,
    sponge_in,
    fb_out,
    fa_out,
    ab_out,
    aa_out,
    drift_out,
    spread_out,
    sources,
    wavelet,
    receivers,
    misfit,
    sponge,
    S,
    vel,
    bpad,
    C,
    damp,
    src_hot,
    inj,
    b_parts,
    hot,
    fade_speed,
    grad_scale,
    base,
    grad,
    mcols,
    gcols,
    mix_m,
    mix_g,
    T,
    KB,
    gram_px,
    gram_py,
    gram_dom,
    norm_px,
    norm_py,
    norm_dom,
    load_sem,
    halo_send,
    halo_recv,
    col_send,
    col_recv,
    sum_send,
    sum_recv,
):
    n_px, n_py, n_dom = counts
    parts, size_x, size_y, size_z = vel.shape
    steps = wavelet.shape[1]
    tiles = size_y // 8
    px, py, dom = lax.axis_index("px"), lax.axis_index("py"), lax.axis_index("dom")
    coord = {"px": px, "py": py, "dom": dom}
    count = {"px": n_px, "py": n_py, "dom": n_dom}
    total_x, total_y = size_x * n_px, size_y * n_py
    particles = parts * n_dom
    share = size_x // n_dom
    cells = pl.ds(EDGE, size_x), pl.ds(TOP, size_y)
    row8 = lax.broadcasted_iota(jnp.int32, (8, size_z), 0)
    lane8 = lax.broadcasted_iota(jnp.int32, (8, size_z), 1)

    def peer(axis, k):
        return lax.rem(coord[axis] + k, count[axis])

    barrier = pltpu.get_barrier_semaphore()
    for axis in ("px", "py", "dom"):
        for k in range(1, count[axis]):
            pl.semaphore_signal(barrier, inc=1, device_id={axis: peer(axis, k)}, device_id_type=MESH)

    loads = [
        pltpu.make_async_copy(vel_in, vel, load_sem.at[0]),
        pltpu.make_async_copy(buoy_in, bpad.at[cells], load_sem.at[1]),
        pltpu.make_async_copy(fn_in, S.at[(1, pl.ds(0, parts)) + cells], load_sem.at[2]),
        pltpu.make_async_copy(an_in, S.at[(1, pl.ds(parts, parts)) + cells], load_sem.at[3]),
        pltpu.make_async_copy(fp_in, S.at[(0, pl.ds(0, parts)) + cells], load_sem.at[4]),
        pltpu.make_async_copy(ap_in, S.at[(0, pl.ds(parts, parts)) + cells], load_sem.at[5]),
    ]
    small = (
        (sources_in, sources),
        (wavelet_in, wavelet),
        (receivers_in, receivers),
        (misfit_in, misfit),
        (sponge_in, sponge),
    )
    for at, (src, dst) in enumerate(small):
        loads.append(pltpu.make_async_copy(src, dst, load_sem.at[6 + at]))
    for copy in loads:
        copy.start()

    zero_rows = jnp.zeros((8, size_z), F32)
    zero_plane = jnp.zeros((size_y, size_z), F32)

    def zero_planes(first):
        for k in range(EDGE):
            bpad[first + k, pl.ds(TOP, size_y), :] = zero_plane
            for state in range(1, 1 + steps):
                for f in range(2 * parts):
                    S[state, f, first + k, pl.ds(TOP, size_y), :] = zero_plane

    def zero_strip(first):
        def body(x, carry):
            bpad[x, pl.ds(first, 8), :] = zero_rows
            for state in range(1, 1 + steps):
                for f in range(2 * parts):
                    S[state, f, x, pl.ds(first, 8), :] = zero_rows
            return carry

        lax.fori_loop(EDGE, EDGE + size_x, body, 0)

    pl.when(px == 0)(lambda: zero_planes(0))
    pl.when(px == n_px - 1)(lambda: zero_planes(EDGE + size_x))
    pl.when(py == 0)(lambda: zero_strip(0))
    pl.when(py == n_py - 1)(lambda: zero_strip(TOP + size_y))

    def halo_copies(ref, lead, group):
        def at(x, y):
            return ref.at[lead + (x, y)]

        x_all, y_all = cells
        last_x, last_y = EDGE + size_x, TOP + size_y
        moves = (
            ("px", 1, at(pl.ds(last_x - EDGE, EDGE), y_all), at(pl.ds(0, EDGE), y_all)),
            ("px", -1, at(pl.ds(EDGE, EDGE), y_all), at(pl.ds(last_x, EDGE), y_all)),
            ("py", 1, at(x_all, pl.ds(last_y - EDGE, EDGE)), at(x_all, pl.ds(TOP - EDGE, EDGE))),
            ("py", -1, at(x_all, pl.ds(TOP, EDGE)), at(x_all, pl.ds(last_y, EDGE))),
        )
        copies = []
        for way, (axis, k, src, dst) in enumerate(moves):
            copies.append(
                pltpu.make_async_remote_copy(
                    src,
                    dst,
                    halo_send.at[group, way],
                    halo_recv.at[group, way],
                    device_id={axis: peer(axis, k + count[axis])},
                    device_id_type=MESH,
                )
            )
        can_send = (px < n_px - 1, px > 0, py < n_py - 1, py > 0)
        can_recv = (px > 0, px < n_px - 1, py > 0, py < n_py - 1)
        return copies, can_send, can_recv

    def send_halo(halo):
        copies, can_send, _ = halo
        for way in (2, 3, 0, 1):
            pl.when(can_send[way])(copies[way].start)

    def wait_halo(halo):
        copies, can_send, can_recv = halo
        for way in range(4):
            pl.when(can_send[way])(copies[way].wait_send)
            pl.when(can_recv[way])(copies[way].wait_recv)

    halo_b = halo_copies(bpad, (), 0)
    halo_w = {
        (state, kind): halo_copies(S, (state, pl.ds(kind * parts, parts)), 2 * state - 1 + kind)
        for state in range(1, 1 + steps)
        for kind in range(2)
    }

    def column_copies(values, cols, lane):
        return [
            pltpu.make_async_remote_copy(
                values.at[:, pl.ds(peer("dom", k) * share, share)],
                cols.at[pl.ds(dom * parts, parts)],
                col_send.at[lane, k],
                col_recv.at[lane, k],
                device_id={"dom": peer("dom", k)},
                device_id_type=MESH,
            )
            for k in range(1, n_dom)
        ]

    def own_column(values, cols, lane):
        return pltpu.make_async_copy(
            values.at[:, pl.ds(dom * share, share)], cols.at[pl.ds(dom * parts, parts)], col_send.at[lane, 0]
        )

    slots = []
    for _ in range(2):
        for axis in ("px", "py", "dom"):
            slots.append(axis)

    def sum_copies(buffer, axis, slot):
        return [
            pltpu.make_async_remote_copy(
                buffer.at[coord[axis]],
                buffer.at[coord[axis]],
                sum_send.at[slot, k],
                sum_recv.at[slot, k],
                device_id={axis: peer(axis, k)},
                device_id_type=MESH,
            )
            for k in range(1, count[axis])
        ]

    def sum_send_off(buffer, axis, slot, value):
        buffer[coord[axis]] = value
        for copy in sum_copies(buffer, axis, slot):
            copy.start()

    def sum_gather(buffer, axis, slot):
        for copy in sum_copies(buffer, axis, slot):
            copy.wait()
        value = buffer[0]
        for k in range(1, count[axis]):
            value = value + buffer[k]
        return value

    def pre_step(step, kind):
        now, before = step + 1, step

        def plane(x, carry):
            for t in range(tiles):
                rows, wide = pl.ds(8 * t, 8), pl.ds(TOP + 8 * t, 8)
                weights = [C[k, x, rows, :] for k in (0, 13, 14, 15, 16, 17, 18)]
                fade = damp[x, rows, :]
                for p in range(parts):
                    f = kind * parts + p
                    here = S[now, f, x + EDGE, wide, :]
                    old = S[before, f, x + EDGE, wide, :]
                    lap = weights[0] * here
                    for k, weight in zip(SHIFTS, weights[1:]):
                        lap = lap + weight * pltpu.roll(here, (size_z - k) % size_z, 1)
                    if kind == 0:
                        add = src_hot[p, x, rows, :] * (STEP_SQ * wavelet[p, step])
                    else:
                        add = inj[step, p, pl.ds(pl.multiple_of(x * size_y, size_y) + 8 * t, 8), :]
                    base[kind, p, x, rows, :] = fade_speed[p, x, rows, :] * lap + fade * ((here + here) - old + add)
                    if kind == 0 and step > 0:
                        older = S[before - 1, f, x + EDGE, wide, :]
                        part = S[before, parts + p, x + EDGE, wide, :] * ((here - (old + old)) + older)
                        if step > 1:
                            part = part + grad[p, x, rows, :]
                        grad[p, x, rows, :] = part
            return carry

        lax.fori_loop(0, size_x, plane, 0, unroll=2)

    def post_step(step, kind):
        now, before, later = step + 1, step, step + 2
        last = step == steps - 1

        def plane(x, carry):
            sums = list(carry)
            for t in range(tiles):
                rows, wide = pl.ds(8 * t, 8), pl.ds(TOP + 8 * t, 8)
                weights = [C[1 + k, x, rows, :] for k in range(12)] + [C[19, x, rows, :]]
                for p in range(parts):
                    f = kind * parts + p
                    lap = weights[12] * S[now, f, x + EDGE, wide, :]
                    for k, weight in zip(SHIFTS, weights[:6]):
                        lap = lap + weight * S[now, f, x + EDGE + k, wide, :]
                    for k, weight in zip(SHIFTS, weights[6:12]):
                        lap = lap + weight * S[now, f, x + EDGE, pl.ds(TOP + 8 * t + k, 8), :]
                    new = base[kind, p, x, rows, :] + fade_speed[p, x, rows, :] * lap
                    if not last:
                        S[later, f, x + EDGE, wide, :] = new
                    if step >= steps - 2:
                        results[kind][step - steps + 2][p, x, rows, :] = new
                    if kind == 0 and last:
                        here = S[now, f, x + EDGE, wide, :]
                        bend = (new - (here + here)) + S[before, f, x + EDGE, wide, :]
                        part = S[now, parts + p, x + EDGE, wide, :] * bend
                        if step > 0:
                            part = part + grad[p, x, rows, :]
                        part = part * grad_scale[p, x, rows, :]
                        sums[p] = sums[p] + part * part
                        grad[p, x, rows, :] = part
            return tuple(sums)

        start = tuple(jnp.zeros((8, size_z), F32) for _ in range(parts)) if kind == 0 and last else ()
        return lax.fori_loop(0, size_x, plane, start, unroll=2)

    results = ((fb_out, fa_out), (ab_out, aa_out))

    for copy in loads[:4]:
        copy.wait()
    pl.semaphore_wait(barrier, (n_px - 1) + (n_py - 1) + (n_dom - 1))
    send_halo(halo_b)
    send_halo(halo_w[1, 0])
    send_halo(halo_w[1, 1])
    model_moves = column_copies(vel, mcols, 0)
    for copy in model_moves:
        copy.start()
    model_own = own_column(vel, mcols, 0)
    model_own.start()

    for copy in loads[6:]:
        copy.wait()

    widths = [sponge[k].astype(F32) for k in range(6)]
    base_x, base_y = px * size_x, py * size_y
    fade_yz = [
        sponge_part((row8 + (8 * t + base_y)).astype(F32), float(total_y), widths[2], widths[3])
        + sponge_part(lane8.astype(F32), float(size_z), widths[4], widths[5])
        for t in range(tiles)
    ]

    def tables(x, carry):
        at_x = jnp.full((8, size_z), x + base_x, jnp.int32)
        fade_x = sponge_part(at_x.astype(F32), float(total_x), widths[0], widths[1])
        for t in range(tiles):
            rows = pl.ds(8 * t, 8)
            damp[x, rows, :] = jnp.exp(-(fade_x + fade_yz[t]))
            flat = (at_x * total_y + (row8 + (8 * t + base_y))) * size_z + lane8
            for p in range(parts):
                speed = vel[p, x, rows, :]
                square = speed * speed
                fade_speed[p, x, rows, :] = damp[x, rows, :] * square
                grad_scale[p, x, rows, :] = -2.0 / (square * speed)
                src_hot[p, x, rows, :] = jnp.where(flat == sources[p], 1.0, 0.0)
        return carry

    lax.fori_loop(0, size_x, tables, 0)

    z_bits, y_bits = size_z.bit_length() - 1, total_y.bit_length() - 1
    n_recv = receivers.shape[1]
    row16 = lax.broadcasted_iota(jnp.int32, (16, n_recv), 0)

    def inject(p):
        index = receivers[pl.ds(p, 1), :]
        local_x = (index >> (z_bits + y_bits)) - base_x
        local_y = ((index >> z_bits) & (total_y - 1)) - base_y
        inside = (local_x >= 0) & (local_x < size_x) & (local_y >= 0) & (local_y < size_y)
        at_plane = jnp.where(inside, local_x * size_y + local_y, -1) - row16
        depth = (index & (size_z - 1)) - row16
        amounts = []
        for s in range(steps):
            amount = STEP_SQ * misfit[s, pl.ds(p, 1), :]
            high = amount.astype(BF16).astype(F32)
            amounts += [high, amount - high]

        def depths(m, carry):
            hit = depth == m * 16
            for k, amount in enumerate(amounts):
                b_parts[k, pl.ds(pl.multiple_of(m * 16, 16), 16), :] = jnp.where(hit, amount, 0.0).astype(BF16)
            return carry

        lax.fori_loop(0, size_z // 16, depths, 0)

        def planes(m, carry):
            hot[pl.ds(pl.multiple_of(m * 16, 16), 16), :] = jnp.where(at_plane == m * 16, 1.0, 0.0).astype(BF16)
            return carry

        lax.fori_loop(0, size_x * size_y // 16, planes, 0, unroll=2)
        for s in range(steps):
            both = lax.dot_general(
                hot[...],
                b_parts[pl.ds(2 * s, 2)].reshape(2 * size_z, n_recv),
                NT,
                preferred_element_type=F32,
            )
            inj[s, p] = both[:, :size_z] + both[:, size_z:]


    def face_weights(around, scale):
        return axis_coefs([scale * (around[k] + around[k + 1]) for k in (-2, -1, 0, 1)])

    def stencil_z(x, carry):
        for t in range(tiles):
            rows = pl.ds(8 * t, 8)
            here = bpad[x + EDGE, pl.ds(TOP + 8 * t, 8), :]
            around = {0: here}
            for k in (-2, -1, 1, 2):
                around[k] = jnp.where(within[k], pltpu.roll(here, (size_z - k) % size_z, 1), 0.0)
            weights = face_weights(around, (0.5 * STEP_SQ) / here)
            C[0, x, rows, :] = weights[0]
            for at, (k, weight) in enumerate(zip(SHIFTS, weights[1:])):
                C[13 + at, x, rows, :] = jnp.where(within[k], weight, 0.0)
        return carry

    def stencil_xy(x, carry):
        for t in range(tiles):
            rows = pl.ds(8 * t, 8)
            here = bpad[x + EDGE, pl.ds(TOP + 8 * t, 8), :]
            scale = (0.5 * STEP_SQ) / here
            at_x = {k: bpad[x + EDGE + k, pl.ds(TOP + 8 * t, 8), :] for k in range(-2, 3)}
            at_y = {k: bpad[x + EDGE, pl.ds(TOP + 8 * t + k, 8), :] for k in range(-2, 3)}
            along_x, along_y = face_weights(at_x, scale), face_weights(at_y, scale)
            C[19, x, rows, :] = along_x[0] + along_y[0]
            for at in range(6):
                C[1 + at, x, rows, :] = along_x[1 + at]
                C[7 + at, x, rows, :] = along_y[1 + at]
        return carry

    within = {k: (lane8 + k >= 0) & (lane8 + k < size_z) for k in SHIFTS}
    lax.fori_loop(0, size_x, stencil_z, 0)
    for copy in loads[4:6]:
        copy.wait()
    pre_step(0, 0)
    inject(0)
    wait_halo(halo_b)
    lax.fori_loop(0, size_x, stencil_xy, 0)

    wait_halo(halo_w[1, 0])
    post_step(0, 0)
    send_halo(halo_w[2, 0])
    for p in range(1, parts):
        inject(p)
    pre_step(0, 1)
    wait_halo(halo_w[1, 1])
    post_step(0, 1)
    send_halo(halo_w[2, 1])
    pre_step(1, 0)
    wait_halo(halo_w[2, 0])
    post_step(1, 0)
    send_halo(halo_w[3, 0])
    pre_step(2, 0)

    model_own.wait()
    for copy in model_moves:
        copy.wait()
    blocks = [(a, pl.ds(8 * t, 8)) for a in range(share) for t in range(tiles)]

    half = particles // 2
    T[...] = jnp.zeros_like(T)

    def distances(i, carry):
        mine = [mcols[i, a, rows, :] for a, rows in blocks]
        for k in range(1, half + 1):
            j = lax.rem(i + k, particles)
            total = None
            for value, (a, rows) in zip(mine, blocks):
                gap = value - mcols[j, a, rows, :]
                total = gap * gap if total is None else total + gap * gap
            T[i, pl.ds(k, 1), :] = jnp.sum(total, axis=0, keepdims=True)
        return carry

    lax.fori_loop(0, particles, distances, 0)
    pairs = particles * particles
    lane_sums = lax.dot_general(
        jnp.ones((8, size_z), F32),
        T[...].reshape(pairs, size_z),
        NT,
        precision=HIGHEST,
        preferred_element_type=F32,
    )
    gram = jnp.where(row8 == 0, lane_sums[:, :128], lane_sums[:, 128:])
    sum_send_off(gram_dom, "dom", 2, gram)
    pre_step(1, 1)
    wait_halo(halo_w[2, 1])
    post_step(1, 1)
    send_halo(halo_w[3, 1])

    wait_halo(halo_w[3, 0])
    grad_sums = post_step(2, 0)
    grad_moves = column_copies(grad, gcols, 1)
    for copy in grad_moves:
        copy.start()
    grad_own = own_column(grad, gcols, 1)
    grad_own.start()
    norm = jnp.zeros((8, size_z), F32)
    for p in range(parts):
        norm = jnp.where(lane8 % particles == dom * parts + p, jnp.sum(grad_sums[p]), norm)
    sum_send_off(norm_px, "px", 3, norm)
    gram = sum_gather(gram_dom, "dom", 2)
    sum_send_off(gram_px, "px", 0, gram)
    norm = sum_gather(norm_px, "px", 3)
    sum_send_off(norm_py, "py", 4, norm)
    gram = sum_gather(gram_px, "px", 0)
    sum_send_off(gram_py, "py", 1, gram)

    pre_step(2, 1)
    wait_halo(halo_w[3, 1])
    post_step(2, 1)
    norm = sum_gather(norm_py, "py", 4)
    sum_send_off(norm_dom, "dom", 5, norm)
    gram = sum_gather(gram_py, "py", 1)

    twice = jnp.where(lane8 % particles == half, 1.0, 2.0)
    width = jnp.sum(jnp.where(row8 < 2, gram * twice, 0.0)) / (particles * (particles - 1)) + EPSILON
    weight = jnp.exp(-gram / width)
    square = lax.broadcasted_iota(jnp.int32, (128, 128), 0) == lax.broadcasted_iota(jnp.int32, (128, 128), 1)

    def rows_of(row):
        return jnp.dot(
            jnp.where(square, row, 0.0), jnp.ones((128, size_z), F32), precision=HIGHEST, preferred_element_type=F32
        )

    def back_copy(mixed, out, lane, k, target):
        return pltpu.make_async_remote_copy(
            mixed.at[pl.ds(target * parts, parts)],
            out.at[:, pl.ds(dom * share, share)],
            col_send.at[lane, k],
            col_recv.at[lane, k],
            device_id={"dom": target},
            device_id_type=MESH,
        )

    def mix(cols, mixed, out, sem_lane, model):
        def one(k, carry):
            target = lax.rem(dom + k, n_dom)
            for p in range(parts):
                i = target * parts + p
                others = [lax.rem(i + k, particles) for k in range(particles)]
                factors = [KB[i, pl.ds(k, 1), :] for k in range(half + 1)]
                factors += [KB[others[k], pl.ds(particles - k, 1), :] for k in range(half + 1, particles)]
                if model:
                    row_sum = factors[0]
                    for factor in factors[1:]:
                        row_sum = row_sum + factor
                for a, rows in blocks:
                    total = None
                    for j, factor in zip(others, factors):
                        term = factor * cols[j, a, rows, :]
                        total = term if total is None else total + term
                    if model:
                        total = cols[i, a, rows, :] * row_sum - total
                    mixed[i, a, rows, :] = total
            pl.when(k < n_dom)(lambda: back_copy(mixed, out, sem_lane, lax.rem(k, n_dom), target).start())
            return carry

        lax.fori_loop(1, n_dom + 1, one, 0)
        own = pltpu.make_async_copy(
            mixed.at[pl.ds(dom * parts, parts)], out.at[:, pl.ds(dom * share, share)], col_send.at[sem_lane, 0]
        )
        own.start()
        return own

    for part in range(pairs // 128):
        at = pl.ds(part * 128 // particles, 128 // particles)
        KB[at] = rows_of(weight[part : part + 1, :]).reshape(128 // particles, particles, size_z)
    spread_own = mix(mcols, mix_m, spread_out, 2, True)

    norm = sum_gather(norm_dom, "dom", 5)
    scale = 1.0 / jnp.sqrt(norm / float(total_x * total_y * size_z) + EPSILON)
    T[0] = rows_of(scale[0:1, :])[:particles]
    grad_own.wait()
    for copy in grad_moves:
        copy.wait()
    def divide(j, carry):
        for a, rows in blocks:
            gcols[j, a, rows, :] = gcols[j, a, rows, :] * T[0, pl.ds(j, 1), :]
        return carry

    lax.fori_loop(0, particles, divide, 0)
    drift_own = mix(gcols, mix_g, drift_out, 3, False)

    spread_own.wait()
    drift_own.wait()
    for k in range(1, n_dom):
        back_copy(mix_m, spread_out, 2, k, peer("dom", k)).wait()
    for k in range(1, n_dom):
        back_copy(mix_g, drift_out, 3, k, peer("dom", k)).wait()


def put_out(*refs):
    sem = refs[-1]
    copies = [pltpu.make_async_copy(refs[k].at[p], refs[6 + k].at[p], sem.at[2 * k + p]) for k in range(6) for p in range(2)]
    for copy in copies:
        copy.start()
    for copy in copies:
        copy.wait()


def on_device(counts, *args):
    velocity, wavelet, receivers = args[0], args[7], args[8]
    parts, size_x, size_y, size_z = velocity.shape
    steps, n_recv = wavelet.shape[1], receivers.shape[1]
    n_px, n_py, n_dom = counts
    particles = parts * n_dom
    share = size_x // n_dom
    pad_x, pad_y = size_x + 2 * EDGE, size_y + 2 * TOP
    whole = (parts, size_x, size_y, size_z)
    cols = (particles, share, size_y, size_z)
    most = max(counts)
    hbm = pl.BlockSpec(memory_space=pltpu.HBM)
    vmem = pl.BlockSpec(memory_space=pltpu.VMEM)
    dma = pltpu.SemaphoreType.DMA
    args = args[:9] + (jnp.transpose(args[9], (1, 0, 2)), args[10])
    results = pl.pallas_call(
        functools.partial(kernel, counts),
        out_shape=[pltpu.VMEM(whole, F32)] * 6,
        in_specs=[hbm] * 11,
        out_specs=[vmem] * 6,
        scratch_shapes=[
            pltpu.SMEM((parts,), jnp.int32),
            pltpu.SMEM((parts, steps), F32),
            pltpu.VMEM((parts, n_recv), jnp.int32),
            pltpu.VMEM((steps, parts, n_recv), F32),
            pltpu.SMEM((6,), jnp.int32),
            pltpu.VMEM((steps + 1, 2 * parts, pad_x, pad_y, size_z), F32),
            pltpu.VMEM(whole, F32),
            pltpu.VMEM((pad_x, pad_y, size_z), F32),
            pltpu.VMEM((20, size_x, size_y, size_z), F32),
            pltpu.VMEM((size_x, size_y, size_z), F32),
            pltpu.VMEM(whole, F32),
            pltpu.VMEM((steps, parts, size_x * size_y, size_z), F32),
            pltpu.VMEM((2 * steps, size_z, n_recv), BF16),
            pltpu.VMEM((size_x * size_y, n_recv), BF16),
            pltpu.VMEM(whole, F32),
            pltpu.VMEM(whole, F32),
            pltpu.VMEM((2,) + whole, F32),
            pltpu.VMEM(whole, F32),
            pltpu.VMEM(cols, F32),
            pltpu.VMEM(cols, F32),
            pltpu.VMEM(cols, F32),
            pltpu.VMEM(cols, F32),
            pltpu.VMEM((particles, particles, size_z), F32),
            pltpu.VMEM((particles, particles, size_z), F32),
            pltpu.VMEM((n_px, 8, size_z), F32),
            pltpu.VMEM((n_py, 8, size_z), F32),
            pltpu.VMEM((n_dom, 8, size_z), F32),
            pltpu.VMEM((n_px, 8, size_z), F32),
            pltpu.VMEM((n_py, 8, size_z), F32),
            pltpu.VMEM((n_dom, 8, size_z), F32),
            dma((11,)),
            dma((1 + 2 * steps, 4)),
            dma((1 + 2 * steps, 4)),
            dma((4, n_dom)),
            dma((4, n_dom)),
            dma((6, most)),
            dma((6, most)),
        ],
        compiler_params=pltpu.CompilerParams(collective_id=0, has_side_effects=True, vmem_limit_bytes=40 * 1024 * 1024),
    )(*[pltpu.with_memory_space_constraint(arg, pltpu.HBM) for arg in args])
    results = [pltpu.with_memory_space_constraint(result, pltpu.VMEM) for result in results]
    return pl.pallas_call(
        put_out,
        out_shape=[jax.ShapeDtypeStruct(whole, F32)] * 6,
        in_specs=[vmem] * 6,
        out_specs=[hbm] * 6,
        scratch_shapes=[dma((12,))],
    )(*results)


def solution(mesh):
    counts = (mesh.shape["px"], mesh.shape["py"], mesh.shape["dom"])
    field = P("dom", "px", "py", None)
    return jax.shard_map(
        functools.partial(on_device, counts),
        mesh=mesh,
        in_specs=(
            field,
            P("px", "py", None),
            field,
            field,
            field,
            field,
            P("dom"),
            P("dom", None),
            P("dom", None),
            P("dom", None, None),
            P(),
        ),
        out_specs=(field,) * 6,
        check_vma=False,
    )
```

```python
import functools

import jax
import jax.numpy as jnp
from jax import lax
from jax.experimental import pallas as pl
from jax.experimental.pallas import tpu as pltpu
from jax.sharding import PartitionSpec as P

EPSILON = 1e-06
TIME_STEP = 0.18
STEP_SQ = TIME_STEP * TIME_STEP
SPONGE_RATE = 0.5
NEAR = 9.0 / 8.0
FAR = 1.0 / 24.0
MESH = pl.DeviceIdType.MESH
F32 = jnp.float32
BF16 = jnp.bfloat16
HIGHEST = lax.Precision.HIGHEST
NT = (((1,), (1,)), ((), ()))
EDGE = 3
TOP = 8


def sponge_part(position, length, low, high):
    far_side = (length - 1) - position
    low_part = jnp.where(position < low, jnp.square(SPONGE_RATE * (low - position) / low), 0.0)
    high_part = jnp.where(far_side < high, jnp.square(SPONGE_RATE * (high - far_side) / high), 0.0)
    return low_part + high_part


def axis_coefs(faces):
    below2, below, here, above = faces
    near_sq, cross, far_sq = NEAR * NEAR, NEAR * FAR, FAR * FAR
    return (
        -near_sq * (here + below) - far_sq * (above + below2),
        near_sq * here + cross * (below + above),
        near_sq * below + cross * (here + below2),
        -cross * (here + above),
        -cross * (below + below2),
        far_sq * above,
        far_sq * below2,
    )


SHIFTS = (1, -1, 2, -2, 3, -3)


def kernel(
    counts,
    vel_in,
    buoy_in,
    fp_in,
    fn_in,
    ap_in,
    an_in,
    sources_in,
    wavelet_in,
    receivers_in,
    misfit_in,
    sponge_in,
    fb_out,
    fa_out,
    ab_out,
    aa_out,
    drift_out,
    spread_out,
    sources,
    wavelet,
    receivers,
    misfit,
    sponge,
    S,
    vel,
    bpad,
    C,
    damp,
    src_hot,
    inj,
    b_parts,
    hot,
    fade_speed,
    grad_scale,
    base,
    grad,
    mcols,
    gcols,
    mix_m,
    mix_g,
    T,
    KB,
    gram_core,
    gram_plane,
    gram_dom,
    norm_core,
    norm_plane,
    norm_dom,
    load_sem,
    halo_send,
    halo_recv,
    col_send,
    col_recv,
    sum_send,
    sum_recv,
):
    n_px, n_py, n_dom = counts
    parts, size_x, size_y, size_z = vel.shape
    steps = wavelet.shape[1]
    tiles = size_y // 8
    px, py, dom = lax.axis_index("px"), lax.axis_index("py"), lax.axis_index("dom")
    coord = {"px": px, "py": py, "dom": dom}
    count = {"px": n_px, "py": n_py, "dom": n_dom}
    total_x, total_y = size_x * n_px, size_y * n_py
    particles = parts * n_dom
    share = size_x // n_dom
    cells = pl.ds(EDGE, size_x), pl.ds(TOP, size_y)
    row8 = lax.broadcasted_iota(jnp.int32, (8, size_z), 0)
    lane8 = lax.broadcasted_iota(jnp.int32, (8, size_z), 1)

    def peer(axis, k):
        return lax.rem(coord[axis] + k, count[axis])

    barrier = pltpu.get_barrier_semaphore()
    met = [{axis: peer(axis, k)} for axis in ("px", "py", "dom") for k in range(1, count[axis])]
    met += [{"px": peer("px", 2 * c), "py": peer("py", k)} for c in range(1, n_px // 2) for k in range(1, n_py)]
    for device in met:
        pl.semaphore_signal(barrier, inc=1, device_id=device, device_id_type=MESH)

    loads = [
        pltpu.make_async_copy(vel_in, vel, load_sem.at[0]),
        pltpu.make_async_copy(buoy_in, bpad.at[cells], load_sem.at[1]),
        pltpu.make_async_copy(fn_in, S.at[(1, pl.ds(0, parts)) + cells], load_sem.at[2]),
        pltpu.make_async_copy(an_in, S.at[(1, pl.ds(parts, parts)) + cells], load_sem.at[3]),
        pltpu.make_async_copy(fp_in, S.at[(0, pl.ds(0, parts)) + cells], load_sem.at[4]),
        pltpu.make_async_copy(ap_in, S.at[(0, pl.ds(parts, parts)) + cells], load_sem.at[5]),
    ]
    small = (
        (sources_in, sources),
        (wavelet_in, wavelet),
        (receivers_in, receivers),
        (misfit_in, misfit),
        (sponge_in, sponge),
    )
    for at, (src, dst) in enumerate(small):
        loads.append(pltpu.make_async_copy(src, dst, load_sem.at[6 + at]))
    for at in (1, 2, 3, 0, *range(4, len(loads))):
        loads[at].start()

    zero_rows = jnp.zeros((8, size_z), F32)
    zero_plane = jnp.zeros((size_y, size_z), F32)

    def zero_planes(first):
        for k in range(EDGE):
            bpad[first + k, pl.ds(TOP, size_y), :] = zero_plane
            for state in range(1, 1 + steps):
                for f in range(2 * parts):
                    S[state, f, first + k, pl.ds(TOP, size_y), :] = zero_plane

    def zero_strip(first):
        def body(x, carry):
            bpad[x, pl.ds(first, 8), :] = zero_rows
            for state in range(1, 1 + steps):
                for f in range(2 * parts):
                    S[state, f, x, pl.ds(first, 8), :] = zero_rows
            return carry

        lax.fori_loop(EDGE, EDGE + size_x, body, 0)

    pl.when(px == 0)(lambda: zero_planes(0))
    pl.when(px == n_px - 1)(lambda: zero_planes(EDGE + size_x))
    pl.when(py == 0)(lambda: zero_strip(0))
    pl.when(py == n_py - 1)(lambda: zero_strip(TOP + size_y))

    def halo_copies(ref, lead, group, deep=EDGE):
        def at(x, y):
            return ref.at[lead + (x, y)]

        x_all, y_all = cells
        last_x, last_y = EDGE + size_x, TOP + size_y
        moves = (
            ("px", 1, at(pl.ds(last_x - deep, deep), y_all), at(pl.ds(EDGE - deep, deep), y_all)),
            ("px", -1, at(pl.ds(EDGE, deep), y_all), at(pl.ds(last_x, deep), y_all)),
            ("py", 1, at(x_all, pl.ds(last_y - deep, deep)), at(x_all, pl.ds(TOP - deep, deep))),
            ("py", -1, at(x_all, pl.ds(TOP, deep)), at(x_all, pl.ds(last_y, deep))),
        )
        copies = []
        for way, (axis, k, src, dst) in enumerate(moves):
            copies.append(
                pltpu.make_async_remote_copy(
                    src,
                    dst,
                    halo_send.at[group, way],
                    halo_recv.at[group, way],
                    device_id={axis: peer(axis, k + count[axis])},
                    device_id_type=MESH,
                )
            )
        can_send = (px < n_px - 1, px > 0, py < n_py - 1, py > 0)
        can_recv = (px > 0, px < n_px - 1, py > 0, py < n_py - 1)
        return copies, can_send, can_recv

    def send_halo(halo, ways=(2, 3, 0, 1)):
        copies, can_send, _ = halo
        for way in ways:
            pl.when(can_send[way])(copies[way].start)

    x_ways, y_ways = (0, 1), (2, 3)

    def wait_halo(halo, ways=(0, 1, 2, 3)):
        copies, can_send, can_recv = halo
        for way in ways:
            pl.when(can_send[way])(copies[way].wait_send)
            pl.when(can_recv[way])(copies[way].wait_recv)

    halo_b = halo_copies(bpad, (), 0, EDGE - 1)
    halo_w = {
        (state, kind): halo_copies(S, (state, pl.ds(kind * parts, parts)), 2 * state - 1 + kind)
        for state in range(1, 1 + steps)
        for kind in range(2)
    }

    far_first = sorted(range(1, n_dom), key=lambda k: abs(n_dom - 2 * k))

    def column_copies(values, cols, lane, rows=pl.ds(0, size_y)):
        return [
            pltpu.make_async_remote_copy(
                values.at[:, pl.ds(peer("dom", k) * share, share), rows],
                cols.at[pl.ds(dom * parts, parts), :, rows],
                col_send.at[lane, k],
                col_recv.at[lane, k],
                device_id={"dom": peer("dom", k)},
                device_id_type=MESH,
            )
            for k in far_first
        ]

    def own_column(values, cols, lane, rows=pl.ds(0, size_y)):
        return pltpu.make_async_copy(
            values.at[:, pl.ds(dom * share, share), rows],
            cols.at[pl.ds(dom * parts, parts), :, rows],
            col_send.at[lane, 0],
        )

    def group_of(name):
        if name == "dom":
            return dom, n_dom, lambda k: {"dom": peer("dom", k)}
        if name == "core":
            return lax.rem(px, 2), 2, lambda k: {"px": px + 1 - 2 * lax.rem(px, 2)}
        size = n_px // 2 * n_py
        index = lax.div(px, 2) * n_py + py

        def device(k):
            at = lax.rem(index + k, size)
            return {"px": lax.div(at, n_py) * 2 + lax.rem(px, 2), "py": lax.rem(at, n_py)}

        return index, size, device

    def sum_copies(buffer, name, slot):
        index, size, device = group_of(name)
        return [
            pltpu.make_async_remote_copy(
                buffer.at[index, pl.ds(0, 2)],
                buffer.at[index, pl.ds(0, 2)],
                sum_send.at[slot, k],
                sum_recv.at[slot, k],
                device_id=device(k),
                device_id_type=MESH,
            )
            for k in range(1, size)
        ]

    def sum_send_off(buffer, name, slot, value):
        buffer[group_of(name)[0], pl.ds(0, 2), :] = value
        for copy in sum_copies(buffer, name, slot):
            copy.start()

    def sum_gather(buffer, name, slot):
        for copy in sum_copies(buffer, name, slot):
            copy.wait()
        value = buffer[0, pl.ds(0, 2), :]
        for k in range(1, group_of(name)[1]):
            value = value + buffer[k, pl.ds(0, 2), :]
        return value

    every = tuple(range(tiles))
    inner, outer = every[1:-1], (0, tiles - 1)

    def pre_plane(step, kind, chosen):
        now, before = step + 1, step

        def plane(x, carry):
            for t in chosen:
                rows, wide = pl.ds(8 * t, 8), pl.ds(TOP + 8 * t, 8)
                weights = [C[k, x, rows, :] for k in (0, 13, 14, 15, 16, 17, 18)]
                fade = damp[x, rows, :]
                for p in range(parts):
                    f = kind * parts + p
                    here = S[now, f, x + EDGE, wide, :]
                    old = S[before, f, x + EDGE, wide, :]
                    lap = weights[0] * here
                    for k, weight in zip(SHIFTS, weights[1:]):
                        lap = lap + weight * pltpu.roll(here, (size_z - k) % size_z, 1)
                    if kind == 0:
                        add = src_hot[p, x, rows, :] * (STEP_SQ * wavelet[p, step])
                    else:
                        add = inj[step, p, pl.ds(pl.multiple_of(x * size_y, size_y) + 8 * t, 8), :]
                    base[kind, p, x, rows, :] = fade_speed[p, x, rows, :] * lap + fade * ((here + here) - old + add)
                    if kind == 0 and step > 0:
                        older = S[before - 1, f, x + EDGE, wide, :]
                        part = S[before, parts + p, x + EDGE, wide, :] * ((here - (old + old)) + older)
                        if step > 1:
                            part = part + grad[p, x, rows, :]
                        grad[p, x, rows, :] = part
            return carry

        return plane

    def post_plane(step, kind, chosen):
        now, before, later = step + 1, step, step + 2
        last = step == steps - 1

        def plane(x, carry):
            sums = list(carry)
            for t in chosen:
                rows, wide = pl.ds(8 * t, 8), pl.ds(TOP + 8 * t, 8)
                weights = [C[1 + k, x, rows, :] for k in range(12)] + [C[19, x, rows, :]]
                for p in range(parts):
                    f = kind * parts + p
                    lap = weights[12] * S[now, f, x + EDGE, wide, :]
                    for k, weight in zip(SHIFTS, weights[:6]):
                        lap = lap + weight * S[now, f, x + EDGE + k, wide, :]
                    for k, weight in zip(SHIFTS, weights[6:12]):
                        lap = lap + weight * S[now, f, x + EDGE, pl.ds(TOP + 8 * t + k, 8), :]
                    new = base[kind, p, x, rows, :] + fade_speed[p, x, rows, :] * lap
                    if not last:
                        S[later, f, x + EDGE, wide, :] = new
                    if step >= steps - 2:
                        results[kind][step - steps + 2][p, x, rows, :] = new
                    if kind == 0 and last:
                        here = S[now, f, x + EDGE, wide, :]
                        bend = (new - (here + here)) + S[before, f, x + EDGE, wide, :]
                        part = S[now, parts + p, x + EDGE, wide, :] * bend
                        if step > 0:
                            part = part + grad[p, x, rows, :]
                        part = part * grad_scale[p, x, rows, :]
                        sums[p] = sums[p] + part * part
                        grad[p, x, rows, :] = part
            return tuple(sums)

        return plane

    def pre_step(step, kind, chosen=every):
        lax.fori_loop(0, size_x, pre_plane(step, kind, chosen), 0, unroll=2 * tiles // len(chosen))

    def post_step(step, kind, chosen=every, start=()):
        return lax.fori_loop(0, size_x, post_plane(step, kind, chosen), start, unroll=2 * tiles // len(chosen))

    def post_and_pre(post, pre):
        after, ahead = post_plane(*post, every), pre_plane(*pre, every)

        def plane(x, carry):
            after(x, ())
            ahead(x, 0)
            return carry

        lax.fori_loop(0, size_x, plane, 0, unroll=2)

    results = ((fb_out, fa_out), (ab_out, aa_out))

    pl.semaphore_wait(barrier, len(met))
    model_moves = [*column_copies(vel_in, mcols, 0), own_column(vel_in, mcols, 0)]
    for copy in model_moves:
        copy.start()
    loads[1].wait()
    send_halo(halo_b)
    loads[2].wait()
    send_halo(halo_w[1, 0])
    loads[3].wait()
    send_halo(halo_w[1, 1])
    for copy in [loads[0], *loads[6:]]:
        copy.wait()

    widths = [sponge[k].astype(F32) for k in range(6)]
    base_x, base_y = px * size_x, py * size_y
    fade_yz = [
        sponge_part((row8 + (8 * t + base_y)).astype(F32), float(total_y), widths[2], widths[3])
        + sponge_part(lane8.astype(F32), float(size_z), widths[4], widths[5])
        for t in range(tiles)
    ]

    def tables(x, carry):
        at_x = jnp.full((8, size_z), x + base_x, jnp.int32)
        fade_x = sponge_part(at_x.astype(F32), float(total_x), widths[0], widths[1])
        for t in range(tiles):
            rows = pl.ds(8 * t, 8)
            damp[x, rows, :] = jnp.exp(-(fade_x + fade_yz[t]))
            flat = (at_x * total_y + (row8 + (8 * t + base_y))) * size_z + lane8
            for p in range(parts):
                speed = vel[p, x, rows, :]
                square = speed * speed
                fade_speed[p, x, rows, :] = damp[x, rows, :] * square
                grad_scale[p, x, rows, :] = -2.0 / (square * speed)
                src_hot[p, x, rows, :] = jnp.where(flat == sources[p], 1.0, 0.0)
        return carry

    lax.fori_loop(0, size_x, tables, 0)

    z_bits, y_bits = size_z.bit_length() - 1, total_y.bit_length() - 1
    n_recv = receivers.shape[1]
    row16 = lax.broadcasted_iota(jnp.int32, (16, n_recv), 0)

    def recv_index(p):
        return receivers[pl.ds(p, 1), :]

    def mark_planes(p):
        index = recv_index(p)
        local_x = (index >> (z_bits + y_bits)) - base_x
        local_y = ((index >> z_bits) & (total_y - 1)) - base_y
        inside = (local_x >= 0) & (local_x < size_x) & (local_y >= 0) & (local_y < size_y)
        at_plane = jnp.where(inside, local_x * size_y + local_y, -1) - row16

        def planes(m, carry):
            hot[p, pl.ds(pl.multiple_of(m * 16, 16), 16), :] = jnp.where(at_plane == m * 16, 1.0, 0.0).astype(BF16)
            return carry

        lax.fori_loop(0, size_x * size_y // 16, planes, 0, unroll=2)

    def inject(p, chosen_steps):
        depth = (recv_index(p) & (size_z - 1)) - row16
        amounts = []
        for s in chosen_steps:
            amount = STEP_SQ * misfit[s, pl.ds(p, 1), :]
            high = amount.astype(BF16).astype(F32)
            amounts += [high, amount - high]

        def depths(m, carry):
            hit = depth == m * 16
            at = pl.ds(pl.multiple_of(m * 16, 16), 16)
            for k, amount in enumerate(amounts):
                b_parts[p, k, at, :] = jnp.where(hit, amount, 0.0).astype(BF16)
            return carry

        lax.fori_loop(0, size_z // 16, depths, 0)
        both = lax.dot_general(
            hot[p],
            b_parts[p, pl.ds(0, len(amounts))].reshape(len(amounts) * size_z, n_recv),
            NT,
            preferred_element_type=F32,
        )
        for k, s in enumerate(chosen_steps):
            first = 2 * k * size_z
            inj[s, p] = both[:, first : first + size_z] + both[:, first + size_z : first + 2 * size_z]

    def inject_all(*chosen_steps):
        for p in range(parts):
            inject(p, chosen_steps)

    def face_weights(around, scale):
        return axis_coefs([scale * (around[k] + around[k + 1]) for k in (-2, -1, 0, 1)])

    def stencil_z(x, carry):
        for t in range(tiles):
            rows = pl.ds(8 * t, 8)
            here = bpad[x + EDGE, pl.ds(TOP + 8 * t, 8), :]
            around = {0: here}
            for k in (-2, -1, 1, 2):
                around[k] = jnp.where(within[k], pltpu.roll(here, (size_z - k) % size_z, 1), 0.0)
            weights = face_weights(around, (0.5 * STEP_SQ) / here)
            C[0, x, rows, :] = weights[0]
            for at, (k, weight) in enumerate(zip(SHIFTS, weights[1:])):
                C[13 + at, x, rows, :] = jnp.where(within[k], weight, 0.0)
        return carry

    def stencil_xy(x, carry):
        for t in range(tiles):
            rows = pl.ds(8 * t, 8)
            here = bpad[x + EDGE, pl.ds(TOP + 8 * t, 8), :]
            scale = (0.5 * STEP_SQ) / here
            at_x = {k: bpad[x + EDGE + k, pl.ds(TOP + 8 * t, 8), :] for k in range(-2, 3)}
            at_y = {k: bpad[x + EDGE, pl.ds(TOP + 8 * t + k, 8), :] for k in range(-2, 3)}
            along_x, along_y = face_weights(at_x, scale), face_weights(at_y, scale)
            C[19, x, rows, :] = along_x[0] + along_y[0]
            for at in range(6):
                C[1 + at, x, rows, :] = along_x[1 + at]
                C[7 + at, x, rows, :] = along_y[1 + at]
        return carry

    within = {k: (lane8 + k >= 0) & (lane8 + k < size_z) for k in SHIFTS}
    lax.fori_loop(0, size_x, stencil_z, 0, unroll=4)
    for copy in loads[4:6]:
        copy.wait()
    pre_step(0, 0)
    for p in range(parts):
        mark_planes(p)
    inject_all(0, 1)
    wait_halo(halo_b)
    lax.fori_loop(0, size_x, stencil_xy, 0)

    wait_halo(halo_w[1, 0], x_ways)
    post_step(0, 0, inner)
    wait_halo(halo_w[1, 0], y_ways)
    post_step(0, 0, outer)
    send_halo(halo_w[2, 0])
    pre_step(0, 1)
    wait_halo(halo_w[1, 1])
    post_and_pre((0, 1), (1, 0))
    send_halo(halo_w[2, 1], x_ways + y_ways)
    pre_step(1, 1)
    wait_halo(halo_w[2, 0], x_ways)
    post_step(1, 0, inner)
    wait_halo(halo_w[2, 0], y_ways)
    post_step(1, 0, outer)
    send_halo(halo_w[3, 0], x_ways)
    for copy in model_moves:
        copy.wait()
    blocks = [(a, pl.ds(8 * t, 8)) for a in range(share) for t in range(tiles)]

    half = particles // 2
    T[...] = jnp.zeros_like(T)

    def distances(i, carry):
        mine = [mcols[i, a, rows, :] for a, rows in blocks]
        for k in range(1, half + 1):
            j = lax.rem(i + k, particles)
            total = None
            for value, (a, rows) in zip(mine, blocks):
                gap = value - mcols[j, a, rows, :]
                total = gap * gap if total is None else total + gap * gap
            T[i, pl.ds(k, 1), :] = jnp.sum(total, axis=0, keepdims=True)
        return carry

    lax.fori_loop(0, particles, distances, 0)
    pairs = particles * particles
    lane_sums = lax.dot_general(
        jnp.ones((8, size_z), F32),
        T[...].reshape(pairs, size_z),
        NT,
        precision=HIGHEST,
        preferred_element_type=F32,
    )
    gram = jnp.where(row8 == 0, lane_sums[:, :128], lane_sums[:, 128:])[:2]
    sum_send_off(gram_dom, "dom", 2, gram)

    send_halo(halo_w[3, 0], y_ways)
    pre_step(2, 0, inner)
    wait_halo(halo_w[2, 1], x_ways)
    post_step(1, 1, inner)

    wait_halo(halo_w[3, 0], x_ways)
    grad_sums = post_step(2, 0, inner, tuple(jnp.zeros((8, size_z), F32) for _ in range(parts)))
    grad_moves = []

    def send_grad(lane, rows):
        for copy in [*column_copies(grad, gcols, lane, rows), own_column(grad, gcols, lane, rows)]:
            copy.start()
            grad_moves.append(copy)

    send_grad(1, pl.ds(8, size_y - 16))
    pre_step(2, 0, outer)
    wait_halo(halo_w[2, 1], y_ways)
    post_step(1, 1, outer)
    gram = sum_gather(gram_dom, "dom", 2)
    sum_send_off(gram_core, "core", 0, gram)
    wait_halo(halo_w[3, 0], y_ways)
    grad_sums = post_step(2, 0, outer, grad_sums)
    send_grad(4, pl.ds(0, 8))
    send_grad(5, pl.ds(size_y - 8, 8))
    lane2 = lax.broadcasted_iota(jnp.int32, (2, size_z), 1)
    norm = jnp.zeros((2, size_z), F32)
    for p in range(parts):
        norm = jnp.where(lane2 % particles == dom * parts + p, jnp.sum(grad_sums[p]), norm)
    sum_send_off(norm_core, "core", 3, norm)
    gram = sum_gather(gram_core, "core", 0)
    sum_send_off(gram_plane, "plane", 1, gram)
    norm = sum_gather(norm_core, "core", 3)
    sum_send_off(norm_plane, "plane", 4, norm)
    gram = sum_gather(gram_plane, "plane", 1)

    twice = jnp.where(lane2 % particles == half, 1.0, 2.0)
    width = jnp.sum(gram * twice) / (particles * (particles - 1)) + EPSILON
    weight = jnp.exp(-gram / width)
    square = lax.broadcasted_iota(jnp.int32, (128, 128), 0) == lax.broadcasted_iota(jnp.int32, (128, 128), 1)

    def rows_of(row):
        return jnp.dot(
            jnp.where(square, row, 0.0), jnp.ones((128, size_z), F32), precision=HIGHEST, preferred_element_type=F32
        )

    def back_copy(mixed, out, lane, k, target):
        return pltpu.make_async_remote_copy(
            mixed.at[pl.ds(target * parts, parts)],
            out.at[:, pl.ds(dom * share, share)],
            col_send.at[lane, k],
            col_recv.at[lane, k],
            device_id={"dom": target},
            device_id_type=MESH,
        )

    def mix(cols, mixed, out, sem_lane, model):
        def one(n, carry):
            far = lax.div(n + 1, 2)
            k = n_dom // 2 + jnp.where(lax.rem(n, 2) == 1, -far, far)
            target = lax.rem(dom + k, n_dom)
            for p in range(parts):
                i = target * parts + p
                others = [lax.rem(i + k, particles) for k in range(particles)]
                factors = [KB[i, pl.ds(k, 1), :] for k in range(half + 1)]
                factors += [KB[others[k], pl.ds(particles - k, 1), :] for k in range(half + 1, particles)]
                if model:
                    row_sum = factors[0]
                    for factor in factors[1:]:
                        row_sum = row_sum + factor
                for a, rows in blocks:
                    total = None
                    for j, factor in zip(others, factors):
                        term = factor * cols[j, a, rows, :]
                        total = term if total is None else total + term
                    if model:
                        total = cols[i, a, rows, :] * row_sum - total
                    mixed[i, a, rows, :] = total
            pl.when(k > 0)(lambda: back_copy(mixed, out, sem_lane, k, target).start())
            return carry

        lax.fori_loop(0, n_dom, one, 0)
        own = pltpu.make_async_copy(
            mixed.at[pl.ds(dom * parts, parts)], out.at[:, pl.ds(dom * share, share)], col_send.at[sem_lane, 0]
        )
        own.start()
        return own

    for part in range(pairs // 128):
        at = pl.ds(part * 128 // particles, 128 // particles)
        KB[at] = rows_of(weight[part : part + 1, :]).reshape(128 // particles, particles, size_z)
    norm = sum_gather(norm_plane, "plane", 4)
    sum_send_off(norm_dom, "dom", 5, norm)
    send_halo(halo_w[3, 1])
    spread_own = mix(mcols, mix_m, spread_out, 2, True)

    inject_all(2)
    pre_step(2, 1)

    norm = sum_gather(norm_dom, "dom", 5)
    scale = 1.0 / jnp.sqrt(norm / float(total_x * total_y * size_z) + EPSILON)
    T[0] = rows_of(scale[0:1, :])[:particles]
    for copy in grad_moves:
        copy.wait()
    def divide(j, carry):
        for a, rows in blocks:
            gcols[j, a, rows, :] = gcols[j, a, rows, :] * T[0, pl.ds(j, 1), :]
        return carry

    lax.fori_loop(0, particles, divide, 0)
    drift_own = mix(gcols, mix_g, drift_out, 3, False)

    wait_halo(halo_w[3, 1])
    post_step(2, 1)
    spread_own.wait()
    drift_own.wait()
    for k in range(1, n_dom):
        back_copy(mix_m, spread_out, 2, k, peer("dom", k)).wait()
    for k in range(1, n_dom):
        back_copy(mix_g, drift_out, 3, k, peer("dom", k)).wait()


def put_out(*refs):
    sem = refs[-1]
    copies = [pltpu.make_async_copy(refs[k].at[p], refs[6 + k].at[p], sem.at[2 * k + p]) for k in range(6) for p in range(2)]
    for copy in copies:
        copy.start()
    for copy in copies:
        copy.wait()


def on_device(counts, *args):
    velocity, wavelet, receivers = args[0], args[7], args[8]
    parts, size_x, size_y, size_z = velocity.shape
    steps, n_recv = wavelet.shape[1], receivers.shape[1]
    n_px, n_py, n_dom = counts
    particles = parts * n_dom
    share = size_x // n_dom
    pad_x, pad_y = size_x + 2 * EDGE, size_y + 2 * TOP
    whole = (parts, size_x, size_y, size_z)
    cols = (particles, share, size_y, size_z)
    most = max(n_dom, n_px // 2 * n_py)
    hbm = pl.BlockSpec(memory_space=pltpu.HBM)
    vmem = pl.BlockSpec(memory_space=pltpu.VMEM)
    dma = pltpu.SemaphoreType.DMA
    args = args[:9] + (jnp.transpose(args[9], (1, 0, 2)), args[10])
    results = pl.pallas_call(
        functools.partial(kernel, counts),
        out_shape=[pltpu.VMEM(whole, F32)] * 6,
        in_specs=[hbm] * 11,
        out_specs=[vmem] * 6,
        scratch_shapes=[
            pltpu.SMEM((parts,), jnp.int32),
            pltpu.SMEM((parts, steps), F32),
            pltpu.VMEM((parts, n_recv), jnp.int32),
            pltpu.VMEM((steps, parts, n_recv), F32),
            pltpu.SMEM((6,), jnp.int32),
            pltpu.VMEM((steps + 1, 2 * parts, pad_x, pad_y, size_z), F32),
            pltpu.VMEM(whole, F32),
            pltpu.VMEM((pad_x, pad_y, size_z), F32),
            pltpu.VMEM((20, size_x, size_y, size_z), F32),
            pltpu.VMEM((size_x, size_y, size_z), F32),
            pltpu.VMEM(whole, F32),
            pltpu.VMEM((steps, parts, size_x * size_y, size_z), F32),
            pltpu.VMEM((parts, 2 * steps, size_z, n_recv), BF16),
            pltpu.VMEM((parts, size_x * size_y, n_recv), BF16),
            pltpu.VMEM(whole, F32),
            pltpu.VMEM(whole, F32),
            pltpu.VMEM((2,) + whole, F32),
            pltpu.VMEM(whole, F32),
            pltpu.VMEM(cols, F32),
            pltpu.VMEM(cols, F32),
            pltpu.VMEM(cols, F32),
            pltpu.VMEM(cols, F32),
            pltpu.VMEM((particles, particles, size_z), F32),
            pltpu.VMEM((particles, particles, size_z), F32),
            pltpu.VMEM((2, 8, size_z), F32),
            pltpu.VMEM((n_px // 2 * n_py, 8, size_z), F32),
            pltpu.VMEM((n_dom, 8, size_z), F32),
            pltpu.VMEM((2, 8, size_z), F32),
            pltpu.VMEM((n_px // 2 * n_py, 8, size_z), F32),
            pltpu.VMEM((n_dom, 8, size_z), F32),
            dma((11,)),
            dma((1 + 2 * steps, 4)),
            dma((1 + 2 * steps, 4)),
            dma((6, n_dom)),
            dma((6, n_dom)),
            dma((6, most)),
            dma((6, most)),
        ],
        compiler_params=pltpu.CompilerParams(collective_id=0, has_side_effects=True, vmem_limit_bytes=40 * 1024 * 1024),
    )(*[pltpu.with_memory_space_constraint(arg, pltpu.HBM) for arg in args])
    results = [pltpu.with_memory_space_constraint(result, pltpu.VMEM) for result in results]
    return pl.pallas_call(
        put_out,
        out_shape=[jax.ShapeDtypeStruct(whole, F32)] * 6,
        in_specs=[vmem] * 6,
        out_specs=[hbm] * 6,
        scratch_shapes=[dma((12,))],
    )(*results)


def solution(mesh):
    counts = (mesh.shape["px"], mesh.shape["py"], mesh.shape["dom"])
    field = P("dom", "px", "py", None)
    return jax.shard_map(
        functools.partial(on_device, counts),
        mesh=mesh,
        in_specs=(
            field,
            P("px", "py", None),
            field,
            field,
            field,
            field,
            P("dom"),
            P("dom", None),
            P("dom", None),
            P("dom", None, None),
            P(),
        ),
        out_specs=(field,) * 6,
        check_vma=False,
    )
```

```python
import functools

import jax
import jax.numpy as jnp
from jax import lax
from jax.experimental import pallas as pl
from jax.experimental.pallas import tpu as pltpu
from jax.sharding import PartitionSpec as P

EPSILON = 1e-06
TIME_STEP = 0.18
STEP_SQ = TIME_STEP * TIME_STEP
SPONGE_RATE = 0.5
NEAR = 9.0 / 8.0
FAR = 1.0 / 24.0
MESH = pl.DeviceIdType.MESH
F32 = jnp.float32
BF16 = jnp.bfloat16
HIGHEST = lax.Precision.HIGHEST
NT = (((1,), (1,)), ((), ()))
EDGE = 3
TOP = 8


def sponge_part(position, length, low, high):
    far_side = (length - 1) - position
    low_part = jnp.where(position < low, jnp.square(SPONGE_RATE * (low - position) / low), 0.0)
    high_part = jnp.where(far_side < high, jnp.square(SPONGE_RATE * (high - far_side) / high), 0.0)
    return low_part + high_part


def axis_coefs(faces):
    below2, below, here, above = faces
    near_sq, cross, far_sq = NEAR * NEAR, NEAR * FAR, FAR * FAR
    return (
        -near_sq * (here + below) - far_sq * (above + below2),
        near_sq * here + cross * (below + above),
        near_sq * below + cross * (here + below2),
        -cross * (here + above),
        -cross * (below + below2),
        far_sq * above,
        far_sq * below2,
    )


SHIFTS = (1, -1, 2, -2, 3, -3)


def kernel(
    counts,
    vel_in,
    buoy_in,
    fp_in,
    fn_in,
    ap_in,
    an_in,
    sources_in,
    wavelet_in,
    receivers_in,
    misfit_in,
    sponge_in,
    fb_out,
    fa_out,
    ab_out,
    aa_out,
    drift_out,
    spread_out,
    sources,
    wavelet,
    receivers,
    misfit,
    sponge,
    S,
    vel,
    bpad,
    C,
    damp,
    src_hot,
    inj,
    b_parts,
    hot,
    fade_speed,
    grad_scale,
    base,
    grad,
    mcols,
    gcols,
    mix_m,
    mix_g,
    T,
    KB,
    gram_core,
    gram_plane,
    gram_dom,
    norm_core,
    norm_plane,
    norm_dom,
    load_sem,
    halo_send,
    halo_recv,
    col_send,
    col_recv,
    sum_send,
    sum_recv,
):
    n_px, n_py, n_dom = counts
    parts, size_x, size_y, size_z = vel.shape
    steps = wavelet.shape[1]
    tiles = size_y // 8
    px, py, dom = lax.axis_index("px"), lax.axis_index("py"), lax.axis_index("dom")
    coord = {"px": px, "py": py, "dom": dom}
    count = {"px": n_px, "py": n_py, "dom": n_dom}
    total_x, total_y = size_x * n_px, size_y * n_py
    particles = parts * n_dom
    share = size_x // n_dom
    cells = pl.ds(EDGE, size_x), pl.ds(TOP, size_y)
    row8 = lax.broadcasted_iota(jnp.int32, (8, size_z), 0)
    lane8 = lax.broadcasted_iota(jnp.int32, (8, size_z), 1)

    def peer(axis, k):
        return lax.rem(coord[axis] + k, count[axis])

    barrier = pltpu.get_barrier_semaphore()
    met = [{axis: peer(axis, k)} for axis in ("px", "py", "dom") for k in range(1, count[axis])]
    met += [{"px": peer("px", 2 * c), "py": peer("py", k)} for c in range(1, n_px // 2) for k in range(1, n_py)]
    for device in met:
        pl.semaphore_signal(barrier, inc=1, device_id=device, device_id_type=MESH)

    loads = [
        pltpu.make_async_copy(vel_in, vel, load_sem.at[0]),
        pltpu.make_async_copy(buoy_in, bpad.at[cells], load_sem.at[1]),
        pltpu.make_async_copy(fn_in, S.at[(1, pl.ds(0, parts)) + cells], load_sem.at[2]),
        pltpu.make_async_copy(an_in, S.at[(1, pl.ds(parts, parts)) + cells], load_sem.at[3]),
        pltpu.make_async_copy(fp_in, S.at[(0, pl.ds(0, parts)) + cells], load_sem.at[4]),
        pltpu.make_async_copy(ap_in, S.at[(0, pl.ds(parts, parts)) + cells], load_sem.at[5]),
    ]
    small = (
        (sources_in, sources),
        (wavelet_in, wavelet),
        (receivers_in, receivers),
        (misfit_in, misfit),
        (sponge_in, sponge),
    )
    for at, (src, dst) in enumerate(small):
        loads.append(pltpu.make_async_copy(src, dst, load_sem.at[6 + at]))
    for at in (1, 2, 3, 0, *range(4, len(loads))):
        loads[at].start()

    zero_rows = jnp.zeros((8, size_z), F32)
    zero_plane = jnp.zeros((size_y, size_z), F32)

    def zero_planes(first):
        for k in range(EDGE):
            bpad[first + k, pl.ds(TOP, size_y), :] = zero_plane
            for state in range(1, 1 + steps):
                for f in range(2 * parts):
                    S[state, f, first + k, pl.ds(TOP, size_y), :] = zero_plane

    def zero_strip(first):
        def body(x, carry):
            bpad[x, pl.ds(first, 8), :] = zero_rows
            for state in range(1, 1 + steps):
                for f in range(2 * parts):
                    S[state, f, x, pl.ds(first, 8), :] = zero_rows
            return carry

        lax.fori_loop(EDGE, EDGE + size_x, body, 0)

    pl.when(px == 0)(lambda: zero_planes(0))
    pl.when(px == n_px - 1)(lambda: zero_planes(EDGE + size_x))
    pl.when(py == 0)(lambda: zero_strip(0))
    pl.when(py == n_py - 1)(lambda: zero_strip(TOP + size_y))

    def halo_copies(ref, lead, group, deep=EDGE):
        def at(x, y):
            return ref.at[lead + (x, y)]

        x_all, y_all = cells
        last_x, last_y = EDGE + size_x, TOP + size_y
        moves = (
            ("px", 1, at(pl.ds(last_x - deep, deep), y_all), at(pl.ds(EDGE - deep, deep), y_all)),
            ("px", -1, at(pl.ds(EDGE, deep), y_all), at(pl.ds(last_x, deep), y_all)),
            ("py", 1, at(x_all, pl.ds(last_y - deep, deep)), at(x_all, pl.ds(TOP - deep, deep))),
            ("py", -1, at(x_all, pl.ds(TOP, deep)), at(x_all, pl.ds(last_y, deep))),
        )
        copies = []
        for way, (axis, k, src, dst) in enumerate(moves):
            copies.append(
                pltpu.make_async_remote_copy(
                    src,
                    dst,
                    halo_send.at[group, way],
                    halo_recv.at[group, way],
                    device_id={axis: peer(axis, k + count[axis])},
                    device_id_type=MESH,
                )
            )
        can_send = (px < n_px - 1, px > 0, py < n_py - 1, py > 0)
        can_recv = (px > 0, px < n_px - 1, py > 0, py < n_py - 1)
        return copies, can_send, can_recv

    def send_halo(halo, ways=(2, 3, 0, 1)):
        copies, can_send, _ = halo
        for way in ways:
            pl.when(can_send[way])(copies[way].start)

    x_ways, y_ways = (0, 1), (2, 3)

    def wait_halo(halo, ways=(0, 1, 2, 3)):
        copies, can_send, can_recv = halo
        for way in ways:
            pl.when(can_send[way])(copies[way].wait_send)
            pl.when(can_recv[way])(copies[way].wait_recv)

    halo_b = halo_copies(bpad, (), 0, EDGE - 1)
    halo_w = {
        (state, kind): halo_copies(S, (state, pl.ds(kind * parts, parts)), 2 * state - 1 + kind)
        for state in range(1, 1 + steps)
        for kind in range(2)
    }

    far_first = sorted(range(1, n_dom), key=lambda k: abs(n_dom - 2 * k))

    def column_copies(values, cols, lane, rows=pl.ds(0, size_y)):
        return [
            pltpu.make_async_remote_copy(
                values.at[:, pl.ds(peer("dom", k) * share, share), rows],
                cols.at[pl.ds(dom * parts, parts), :, rows],
                col_send.at[lane, k],
                col_recv.at[lane, k],
                device_id={"dom": peer("dom", k)},
                device_id_type=MESH,
            )
            for k in far_first
        ]

    def own_column(values, cols, lane, rows=pl.ds(0, size_y)):
        return pltpu.make_async_copy(
            values.at[:, pl.ds(dom * share, share), rows],
            cols.at[pl.ds(dom * parts, parts), :, rows],
            col_send.at[lane, 0],
        )

    def group_of(name):
        if name == "dom":
            return dom, n_dom, lambda k: {"dom": peer("dom", k)}
        if name == "core":
            return lax.rem(px, 2), 2, lambda k: {"px": px + 1 - 2 * lax.rem(px, 2)}
        size = n_px // 2 * n_py
        index = lax.div(px, 2) * n_py + py

        def device(k):
            at = lax.rem(index + k, size)
            return {"px": lax.div(at, n_py) * 2 + lax.rem(px, 2), "py": lax.rem(at, n_py)}

        return index, size, device

    def sum_copies(buffer, name, slot):
        index, size, device = group_of(name)
        return [
            pltpu.make_async_remote_copy(
                buffer.at[index, pl.ds(0, 2)],
                buffer.at[index, pl.ds(0, 2)],
                sum_send.at[slot, k],
                sum_recv.at[slot, k],
                device_id=device(k),
                device_id_type=MESH,
            )
            for k in range(1, size)
        ]

    def sum_send_off(buffer, name, slot, value):
        buffer[group_of(name)[0], pl.ds(0, 2), :] = value
        for copy in sum_copies(buffer, name, slot):
            copy.start()

    def sum_gather(buffer, name, slot):
        for copy in sum_copies(buffer, name, slot):
            copy.wait()
        value = buffer[0, pl.ds(0, 2), :]
        for k in range(1, group_of(name)[1]):
            value = value + buffer[k, pl.ds(0, 2), :]
        return value

    every = tuple(range(tiles))
    inner, outer = every[1:-1], (0, tiles - 1)

    def pre_plane(step, kind, chosen):
        now, before = step + 1, step

        def plane(x, carry):
            for t in chosen:
                rows, wide = pl.ds(8 * t, 8), pl.ds(TOP + 8 * t, 8)
                weights = [C[k, x, rows, :] for k in (0, 13, 14, 15, 16, 17, 18)]
                fade = damp[x, rows, :]
                for p in range(parts):
                    f = kind * parts + p
                    here = S[now, f, x + EDGE, wide, :]
                    old = S[before, f, x + EDGE, wide, :]
                    lap = weights[0] * here
                    for k, weight in zip(SHIFTS, weights[1:]):
                        lap = lap + weight * pltpu.roll(here, (size_z - k) % size_z, 1)
                    if kind == 0:
                        add = src_hot[p, x, rows, :] * (STEP_SQ * wavelet[p, step])
                    else:
                        add = inj[step, p, pl.ds(pl.multiple_of(x * size_y, size_y) + 8 * t, 8), :]
                    base[kind, p, x, rows, :] = fade_speed[p, x, rows, :] * lap + fade * ((here + here) - old + add)
                    if kind == 0 and step > 0:
                        older = S[before - 1, f, x + EDGE, wide, :]
                        part = S[before, parts + p, x + EDGE, wide, :] * ((here - (old + old)) + older)
                        if step > 1:
                            part = part + grad[p, x, rows, :]
                        grad[p, x, rows, :] = part
            return carry

        return plane

    def post_plane(step, kind, chosen):
        now, before, later = step + 1, step, step + 2
        last = step == steps - 1

        def plane(x, carry):
            sums = list(carry)
            for t in chosen:
                rows, wide = pl.ds(8 * t, 8), pl.ds(TOP + 8 * t, 8)
                weights = [C[1 + k, x, rows, :] for k in range(12)] + [C[19, x, rows, :]]
                for p in range(parts):
                    f = kind * parts + p
                    lap = weights[12] * S[now, f, x + EDGE, wide, :]
                    for k, weight in zip(SHIFTS, weights[:6]):
                        lap = lap + weight * S[now, f, x + EDGE + k, wide, :]
                    for k, weight in zip(SHIFTS, weights[6:12]):
                        lap = lap + weight * S[now, f, x + EDGE, pl.ds(TOP + 8 * t + k, 8), :]
                    new = base[kind, p, x, rows, :] + fade_speed[p, x, rows, :] * lap
                    if not last:
                        S[later, f, x + EDGE, wide, :] = new
                    if step >= steps - 2:
                        results[kind][step - steps + 2][p, x, rows, :] = new
                    if kind == 0 and last:
                        here = S[now, f, x + EDGE, wide, :]
                        bend = (new - (here + here)) + S[before, f, x + EDGE, wide, :]
                        part = S[now, parts + p, x + EDGE, wide, :] * bend
                        if step > 0:
                            part = part + grad[p, x, rows, :]
                        part = part * grad_scale[p, x, rows, :]
                        sums[p] = sums[p] + part * part
                        grad[p, x, rows, :] = part
            return tuple(sums)

        return plane

    def pre_step(step, kind, chosen=every):
        lax.fori_loop(0, size_x, pre_plane(step, kind, chosen), 0, unroll=2 * tiles // len(chosen))

    def post_step(step, kind, chosen=every, carry=(), spans=((0, size_x),)):
        for first, end in spans:
            carry = lax.fori_loop(first, end, post_plane(step, kind, chosen), carry, unroll=2 * tiles // len(chosen))
        return carry

    def post_and_pre(post, pre):
        after, ahead = post_plane(*post, every), pre_plane(*pre, every)

        def plane(x, carry):
            after(x, ())
            ahead(x, 0)
            return carry

        lax.fori_loop(0, size_x, plane, 0, unroll=2)

    results = ((fb_out, fa_out), (ab_out, aa_out))

    pl.semaphore_wait(barrier, len(met))
    model_moves = [*column_copies(vel_in, mcols, 0), own_column(vel_in, mcols, 0)]
    for copy in model_moves:
        copy.start()
    loads[1].wait()
    send_halo(halo_b)
    loads[2].wait()
    send_halo(halo_w[1, 0])
    loads[3].wait()
    send_halo(halo_w[1, 1])
    for copy in [loads[0], *loads[6:]]:
        copy.wait()

    widths = [sponge[k].astype(F32) for k in range(6)]
    base_x, base_y = px * size_x, py * size_y
    fade_yz = [
        sponge_part((row8 + (8 * t + base_y)).astype(F32), float(total_y), widths[2], widths[3])
        + sponge_part(lane8.astype(F32), float(size_z), widths[4], widths[5])
        for t in range(tiles)
    ]

    def tables(x, carry):
        at_x = jnp.full((8, size_z), x + base_x, jnp.int32)
        fade_x = sponge_part(at_x.astype(F32), float(total_x), widths[0], widths[1])
        for t in range(tiles):
            rows = pl.ds(8 * t, 8)
            damp[x, rows, :] = jnp.exp(-(fade_x + fade_yz[t]))
            flat = (at_x * total_y + (row8 + (8 * t + base_y))) * size_z + lane8
            for p in range(parts):
                speed = vel[p, x, rows, :]
                square = speed * speed
                fade_speed[p, x, rows, :] = damp[x, rows, :] * square
                grad_scale[p, x, rows, :] = -2.0 / (square * speed)
                src_hot[p, x, rows, :] = jnp.where(flat == sources[p], 1.0, 0.0)
        return carry

    lax.fori_loop(0, size_x, tables, 0)

    z_bits, y_bits = size_z.bit_length() - 1, total_y.bit_length() - 1
    n_recv = receivers.shape[1]
    row16 = lax.broadcasted_iota(jnp.int32, (16, n_recv), 0)

    def recv_index(p):
        return receivers[pl.ds(p, 1), :]

    def mark_planes(p):
        index = recv_index(p)
        local_x = (index >> (z_bits + y_bits)) - base_x
        local_y = ((index >> z_bits) & (total_y - 1)) - base_y
        inside = (local_x >= 0) & (local_x < size_x) & (local_y >= 0) & (local_y < size_y)
        at_plane = jnp.where(inside, local_x * size_y + local_y, -1) - row16

        def planes(m, carry):
            hot[p, pl.ds(pl.multiple_of(m * 16, 16), 16), :] = jnp.where(at_plane == m * 16, 1.0, 0.0).astype(BF16)
            return carry

        lax.fori_loop(0, size_x * size_y // 16, planes, 0, unroll=2)

    def inject(p, chosen_steps):
        depth = (recv_index(p) & (size_z - 1)) - row16
        amounts = []
        for s in chosen_steps:
            amount = STEP_SQ * misfit[s, pl.ds(p, 1), :]
            high = amount.astype(BF16).astype(F32)
            amounts += [high, amount - high]

        def depths(m, carry):
            hit = depth == m * 16
            at = pl.ds(pl.multiple_of(m * 16, 16), 16)
            for k, amount in enumerate(amounts):
                b_parts[p, k, at, :] = jnp.where(hit, amount, 0.0).astype(BF16)
            return carry

        lax.fori_loop(0, size_z // 16, depths, 0)
        both = lax.dot_general(
            hot[p],
            b_parts[p, pl.ds(0, len(amounts))].reshape(len(amounts) * size_z, n_recv),
            NT,
            preferred_element_type=F32,
        )
        for k, s in enumerate(chosen_steps):
            first = 2 * k * size_z
            inj[s, p] = both[:, first : first + size_z] + both[:, first + size_z : first + 2 * size_z]

    def inject_all(*chosen_steps):
        for p in range(parts):
            inject(p, chosen_steps)

    def face_weights(around, scale):
        return axis_coefs([scale * (around[k] + around[k + 1]) for k in (-2, -1, 0, 1)])

    def stencil_z(x, carry):
        for t in range(tiles):
            rows = pl.ds(8 * t, 8)
            here = bpad[x + EDGE, pl.ds(TOP + 8 * t, 8), :]
            around = {0: here}
            for k in (-2, -1, 1, 2):
                around[k] = jnp.where(within[k], pltpu.roll(here, (size_z - k) % size_z, 1), 0.0)
            weights = face_weights(around, (0.5 * STEP_SQ) / here)
            C[0, x, rows, :] = weights[0]
            for at, (k, weight) in enumerate(zip(SHIFTS, weights[1:])):
                C[13 + at, x, rows, :] = jnp.where(within[k], weight, 0.0)
        return carry

    def stencil_xy(x, carry):
        for t in range(tiles):
            rows = pl.ds(8 * t, 8)
            here = bpad[x + EDGE, pl.ds(TOP + 8 * t, 8), :]
            scale = (0.5 * STEP_SQ) / here
            at_x = {k: bpad[x + EDGE + k, pl.ds(TOP + 8 * t, 8), :] for k in range(-2, 3)}
            at_y = {k: bpad[x + EDGE, pl.ds(TOP + 8 * t + k, 8), :] for k in range(-2, 3)}
            along_x, along_y = face_weights(at_x, scale), face_weights(at_y, scale)
            C[19, x, rows, :] = along_x[0] + along_y[0]
            for at in range(6):
                C[1 + at, x, rows, :] = along_x[1 + at]
                C[7 + at, x, rows, :] = along_y[1 + at]
        return carry

    within = {k: (lane8 + k >= 0) & (lane8 + k < size_z) for k in SHIFTS}
    lax.fori_loop(0, size_x, stencil_z, 0, unroll=4)
    for copy in loads[4:6]:
        copy.wait()
    pre_step(0, 0)
    for p in range(parts):
        mark_planes(p)
    inject_all(0, 1)
    wait_halo(halo_b)
    lax.fori_loop(0, size_x, stencil_xy, 0)

    wait_halo(halo_w[1, 0], x_ways)
    post_step(0, 0, inner)
    wait_halo(halo_w[1, 0], y_ways)
    post_step(0, 0, outer)
    send_halo(halo_w[2, 0])
    pre_step(0, 1)
    wait_halo(halo_w[1, 1])
    post_and_pre((0, 1), (1, 0))
    send_halo(halo_w[2, 1], x_ways + y_ways)
    pre_step(1, 1)
    wait_halo(halo_w[2, 0], x_ways)
    post_step(1, 0, inner)
    wait_halo(halo_w[2, 0], y_ways)
    post_step(1, 0, outer)
    send_halo(halo_w[3, 0], x_ways)
    for copy in model_moves:
        copy.wait()
    blocks = [(a, pl.ds(8 * t, 8)) for a in range(share) for t in range(tiles)]

    half = particles // 2
    T[...] = jnp.zeros_like(T)

    def distances(i, carry):
        mine = [mcols[i, a, rows, :] for a, rows in blocks]
        for k in range(1, half + 1):
            j = lax.rem(i + k, particles)
            total = None
            for value, (a, rows) in zip(mine, blocks):
                gap = value - mcols[j, a, rows, :]
                total = gap * gap if total is None else total + gap * gap
            T[i, pl.ds(k, 1), :] = jnp.sum(total, axis=0, keepdims=True)
        return carry

    lax.fori_loop(0, particles, distances, 0)
    pairs = particles * particles
    lane_sums = lax.dot_general(
        jnp.ones((8, size_z), F32),
        T[...].reshape(pairs, size_z),
        NT,
        precision=HIGHEST,
        preferred_element_type=F32,
    )
    gram = jnp.where(row8 == 0, lane_sums[:, :128], lane_sums[:, 128:])[:2]
    sum_send_off(gram_dom, "dom", 2, gram)

    send_halo(halo_w[3, 0], y_ways)
    pre_step(2, 0, inner)
    low = -(-EDGE // share) * share
    middle, ends = ((low, size_x - low),), ((0, low), (size_x - low, size_x))
    post_step(1, 1, inner, (), middle)
    grad_sums = post_step(2, 0, inner, tuple(jnp.zeros((8, size_z), F32) for _ in range(parts)), middle)
    grad_moves = []

    def grad_copies(lane, rows):
        copies = column_copies(grad, gcols, lane, rows)
        grad_moves.extend([*copies, own_column(grad, gcols, lane, rows)])
        return copies, grad_moves[-1]

    half_moves, half_own = grad_copies(1, pl.ds(8, size_y - 16))
    mid_owner = []
    for copy, k in zip(half_moves, far_first):
        target = peer("dom", k)
        mid_owner.append((target >= low // share) & (target < n_dom - low // share))
        pl.when(mid_owner[-1])(copy.start)
    wait_halo(halo_w[2, 1], x_ways)
    post_step(1, 1, inner, (), ends)
    wait_halo(halo_w[3, 0], x_ways)
    grad_sums = post_step(2, 0, inner, grad_sums, ends)
    for copy, owner in zip(half_moves, mid_owner):
        pl.when(jnp.logical_not(owner))(copy.start)
    half_own.start()
    gram = sum_gather(gram_dom, "dom", 2)
    sum_send_off(gram_core, "core", 0, gram)
    pre_step(2, 0, outer)
    wait_halo(halo_w[2, 1], y_ways)
    post_step(1, 1, outer)
    wait_halo(halo_w[3, 0], y_ways)
    grad_sums = post_step(2, 0, outer, grad_sums)
    for lane, first in ((4, 0), (5, size_y - 8)):
        copies, own = grad_copies(lane, pl.ds(first, 8))
        for copy in [*copies, own]:
            copy.start()
    lane2 = lax.broadcasted_iota(jnp.int32, (2, size_z), 1)
    norm = jnp.zeros((2, size_z), F32)
    for p in range(parts):
        norm = jnp.where(lane2 % particles == dom * parts + p, jnp.sum(grad_sums[p]), norm)
    sum_send_off(norm_core, "core", 3, norm)
    gram = sum_gather(gram_core, "core", 0)
    sum_send_off(gram_plane, "plane", 1, gram)
    norm = sum_gather(norm_core, "core", 3)
    sum_send_off(norm_plane, "plane", 4, norm)
    gram = sum_gather(gram_plane, "plane", 1)

    twice = jnp.where(lane2 % particles == half, 1.0, 2.0)
    width = jnp.sum(gram * twice) / (particles * (particles - 1)) + EPSILON
    weight = jnp.exp(-gram / width)
    square = lax.broadcasted_iota(jnp.int32, (128, 128), 0) == lax.broadcasted_iota(jnp.int32, (128, 128), 1)

    def rows_of(row):
        return jnp.dot(
            jnp.where(square, row, 0.0), jnp.ones((128, size_z), F32), precision=HIGHEST, preferred_element_type=F32
        )

    def back_copy(mixed, out, lane, k, target):
        return pltpu.make_async_remote_copy(
            mixed.at[pl.ds(target * parts, parts)],
            out.at[:, pl.ds(dom * share, share)],
            col_send.at[lane, k],
            col_recv.at[lane, k],
            device_id={"dom": target},
            device_id_type=MESH,
        )

    def mix(cols, mixed, out, sem_lane, model):
        def one(n, carry):
            far = lax.div(n + 1, 2)
            k = n_dom // 2 + jnp.where(lax.rem(n, 2) == 1, -far, far)
            target = lax.rem(dom + k, n_dom)
            for p in range(parts):
                i = target * parts + p
                others = [lax.rem(i + k, particles) for k in range(particles)]
                factors = [KB[i, pl.ds(k, 1), :] for k in range(half + 1)]
                factors += [KB[others[k], pl.ds(particles - k, 1), :] for k in range(half + 1, particles)]
                if model:
                    row_sum = factors[0]
                    for factor in factors[1:]:
                        row_sum = row_sum + factor
                for a, rows in blocks:
                    total = None
                    for j, factor in zip(others, factors):
                        term = factor * cols[j, a, rows, :]
                        total = term if total is None else total + term
                    if model:
                        total = cols[i, a, rows, :] * row_sum - total
                    mixed[i, a, rows, :] = total
            pl.when(k > 0)(lambda: back_copy(mixed, out, sem_lane, k, target).start())
            return carry

        lax.fori_loop(0, n_dom, one, 0)
        own = pltpu.make_async_copy(
            mixed.at[pl.ds(dom * parts, parts)], out.at[:, pl.ds(dom * share, share)], col_send.at[sem_lane, 0]
        )
        own.start()
        return own

    for part in range(pairs // 128):
        at = pl.ds(part * 128 // particles, 128 // particles)
        KB[at] = rows_of(weight[part : part + 1, :]).reshape(128 // particles, particles, size_z)
    norm = sum_gather(norm_plane, "plane", 4)
    sum_send_off(norm_dom, "dom", 5, norm)
    send_halo(halo_w[3, 1])
    spread_own = mix(mcols, mix_m, spread_out, 2, True)

    inject_all(2)
    pre_step(2, 1)

    norm = sum_gather(norm_dom, "dom", 5)
    scale = 1.0 / jnp.sqrt(norm / float(total_x * total_y * size_z) + EPSILON)
    T[0] = rows_of(scale[0:1, :])[:particles]
    for copy in grad_moves:
        copy.wait()
    def divide(j, carry):
        for a, rows in blocks:
            gcols[j, a, rows, :] = gcols[j, a, rows, :] * T[0, pl.ds(j, 1), :]
        return carry

    lax.fori_loop(0, particles, divide, 0)
    drift_own = mix(gcols, mix_g, drift_out, 3, False)

    wait_halo(halo_w[3, 1])
    post_step(2, 1)
    spread_own.wait()
    drift_own.wait()
    for k in range(1, n_dom):
        back_copy(mix_m, spread_out, 2, k, peer("dom", k)).wait()
    for k in range(1, n_dom):
        back_copy(mix_g, drift_out, 3, k, peer("dom", k)).wait()


def put_out(*refs):
    sem = refs[-1]
    copies = [pltpu.make_async_copy(refs[k].at[p], refs[6 + k].at[p], sem.at[2 * k + p]) for k in range(6) for p in range(2)]
    for copy in copies:
        copy.start()
    for copy in copies:
        copy.wait()


def on_device(counts, *args):
    velocity, wavelet, receivers = args[0], args[7], args[8]
    parts, size_x, size_y, size_z = velocity.shape
    steps, n_recv = wavelet.shape[1], receivers.shape[1]
    n_px, n_py, n_dom = counts
    particles = parts * n_dom
    share = size_x // n_dom
    pad_x, pad_y = size_x + 2 * EDGE, size_y + 2 * TOP
    whole = (parts, size_x, size_y, size_z)
    cols = (particles, share, size_y, size_z)
    most = max(n_dom, n_px // 2 * n_py)
    hbm = pl.BlockSpec(memory_space=pltpu.HBM)
    vmem = pl.BlockSpec(memory_space=pltpu.VMEM)
    dma = pltpu.SemaphoreType.DMA
    args = args[:9] + (jnp.transpose(args[9], (1, 0, 2)), args[10])
    results = pl.pallas_call(
        functools.partial(kernel, counts),
        out_shape=[pltpu.VMEM(whole, F32)] * 6,
        in_specs=[hbm] * 11,
        out_specs=[vmem] * 6,
        scratch_shapes=[
            pltpu.SMEM((parts,), jnp.int32),
            pltpu.SMEM((parts, steps), F32),
            pltpu.VMEM((parts, n_recv), jnp.int32),
            pltpu.VMEM((steps, parts, n_recv), F32),
            pltpu.SMEM((6,), jnp.int32),
            pltpu.VMEM((steps + 1, 2 * parts, pad_x, pad_y, size_z), F32),
            pltpu.VMEM(whole, F32),
            pltpu.VMEM((pad_x, pad_y, size_z), F32),
            pltpu.VMEM((20, size_x, size_y, size_z), F32),
            pltpu.VMEM((size_x, size_y, size_z), F32),
            pltpu.VMEM(whole, F32),
            pltpu.VMEM((steps, parts, size_x * size_y, size_z), F32),
            pltpu.VMEM((parts, 2 * steps, size_z, n_recv), BF16),
            pltpu.VMEM((parts, size_x * size_y, n_recv), BF16),
            pltpu.VMEM(whole, F32),
            pltpu.VMEM(whole, F32),
            pltpu.VMEM((2,) + whole, F32),
            pltpu.VMEM(whole, F32),
            pltpu.VMEM(cols, F32),
            pltpu.VMEM(cols, F32),
            pltpu.VMEM(cols, F32),
            pltpu.VMEM(cols, F32),
            pltpu.VMEM((particles, particles, size_z), F32),
            pltpu.VMEM((particles, particles, size_z), F32),
            pltpu.VMEM((2, 8, size_z), F32),
            pltpu.VMEM((n_px // 2 * n_py, 8, size_z), F32),
            pltpu.VMEM((n_dom, 8, size_z), F32),
            pltpu.VMEM((2, 8, size_z), F32),
            pltpu.VMEM((n_px // 2 * n_py, 8, size_z), F32),
            pltpu.VMEM((n_dom, 8, size_z), F32),
            dma((11,)),
            dma((1 + 2 * steps, 4)),
            dma((1 + 2 * steps, 4)),
            dma((6, n_dom)),
            dma((6, n_dom)),
            dma((6, most)),
            dma((6, most)),
        ],
        compiler_params=pltpu.CompilerParams(collective_id=0, has_side_effects=True, vmem_limit_bytes=40 * 1024 * 1024),
    )(*[pltpu.with_memory_space_constraint(arg, pltpu.HBM) for arg in args])
    results = [pltpu.with_memory_space_constraint(result, pltpu.VMEM) for result in results]
    return pl.pallas_call(
        put_out,
        out_shape=[jax.ShapeDtypeStruct(whole, F32)] * 6,
        in_specs=[vmem] * 6,
        out_specs=[hbm] * 6,
        scratch_shapes=[dma((12,))],
    )(*results)


def solution(mesh):
    counts = (mesh.shape["px"], mesh.shape["py"], mesh.shape["dom"])
    field = P("dom", "px", "py", None)
    return jax.shard_map(
        functools.partial(on_device, counts),
        mesh=mesh,
        in_specs=(
            field,
            P("px", "py", None),
            field,
            field,
            field,
            field,
            P("dom"),
            P("dom", None),
            P("dom", None),
            P("dom", None, None),
            P(),
        ),
        out_specs=(field,) * 6,
        check_vma=False,
    )
```
